256 devices in a mesh: dp: 32 (over z, y), ctx: 8 (over x, core).
Axes of the slice: x: 4, y: 4, z: 8, core: 2. Of those that a mesh axis runs over, the one named last changes fastest.
Arguments:
- query_rows: bfloat16 [32768, 4096], P(('dp', 'ctx')), may hold values from -9 to 9
- key_rows: bfloat16 [32768, 1024], P(('dp', 'ctx')), may hold values from -4 to 4
- token_values: bfloat16 [32768, 1024], P(('dp', 'ctx')), may hold values from -6 to 6
- group_of_row: int32 [32768, 1], P(('dp', 'ctx')), may hold values from 0 to 31; in each aligned block of 128 rows (0 to 127, 128 to 255, ...) at most 8 rows name the same one
- doc_lengths: int32 [32, 2], P('dp'), may hold values from 1 to 1536, 2048 in all within a row
Outputs:
- attended: bfloat16 [32768, 4096], P(('dp', 'ctx'))
The draws below stay inside these ranges and needn't reach their ends.
Inputs may be any that keep to these rules, and one draw needn't show every extreme that they name: `group_of_row`: within each device's block of 128 rows no group is named by more than 8 rows; in some blocks one group is named by exactly 8. `doc_lengths`: each group's 2 lengths sum to 2048; neither exceeds 1536.
All inputs are finite; a program needn't handle non-finite values.
Results may differ from the reference program's by a relative error of at most 0.0038.
Values may be sent and summed in bfloat16 or wider, within the bound.
No kernel may reach another device: no remote copies, remote signals or barrier semaphores. Data moves between devices by JAX's collectives and lax.ppermute only.
A program may use at most 128 MiB of HBM per device.

```python
import math
import jax
import jax.numpy as jnp
import numpy as np
from jax import lax

QUERY_HEAD_COUNT = 32
KEY_VALUE_HEADS = 8
HEAD_SIZE = 128
TOK_DEV = 128
DOCS = 2
GROUPS = 32
SLOT = 8
GROUP_ROWS = 2048
DOC_MOST = 1536
TOKEN_ROW_COUNT = 32768


def query_key_pair(key):
    base = jax.random.fold_in(key, 7301)
    random_subkeys = jax.random.split(base, 2)
    rows_per_group = QUERY_HEAD_COUNT // KEY_VALUE_HEADS
    query_matrix = jnp.clip(jax.random.normal(random_subkeys[0], (TOKEN_ROW_COUNT, KEY_VALUE_HEADS, rows_per_group, HEAD_SIZE), jnp.float32), -4.0, 4.0)
    keyed_rows = jnp.clip(jax.random.normal(random_subkeys[1], (TOKEN_ROW_COUNT, KEY_VALUE_HEADS, HEAD_SIZE), jnp.float32), -4.0, 4.0)
    return (query_matrix.reshape(TOKEN_ROW_COUNT, QUERY_HEAD_COUNT * HEAD_SIZE), keyed_rows.reshape(TOKEN_ROW_COUNT, KEY_VALUE_HEADS * HEAD_SIZE))


def draw_query_rows(key, part):
    return query_key_pair(key)[0].astype(jnp.bfloat16)


def draw_key_rows(key, part):
    return query_key_pair(key)[1].astype(jnp.bfloat16)


def steps_of(stream_key, dims, shards, low, largest):
    level = 1.0
    for dim, shards_of in shards:
        heights = jax.random.uniform(jax.random.fold_in(jax.random.fold_in(stream_key, 6), dim), (shards_of,), jnp.float32, low / len(shards), largest / len(shards))
        level = level * jnp.repeat(jnp.exp(heights), dims[dim] // shards_of).reshape((-1,) + (1,) * (len(dims) - 1 - dim))
    return level


def profile(count, total, most, slope):
    loads = [(1 << 20) // math.isqrt(rank ** slope) + 1 for rank in range(2, count + 1)]
    rest, given = total - most - (count - 1), [1] * (count - 1)
    while rest > 0:
        free = [i for i in range(count - 1) if given[i] < most]
        whole, budget = sum([loads[i] for i in free]), rest
        for i in free:
            addition = min(most - given[i], max(1, budget * loads[i] // whole), rest)
            given[i] = given[i] + addition
            rest = rest - addition
    return np.array([most] + given)


def uneven_parts(rng, count, total, reach, skew):
    if count == 2:
        one = jax.random.randint(rng, (), max(1, total - reach), min(reach, total - 1) + 1)
        return jnp.stack([one, total - one])
    tallies = jnp.asarray(profile(count, total, reach, skew), jnp.int32)
    twos = (count - 1) // 2
    giver, sink = tallies[1:1 + 2 * twos:2], tallies[2:2 + 2 * twos:2]
    room = jnp.minimum(giver - 1, reach - sink)
    passed = jax.random.randint(jax.random.fold_in(rng, 1), (twos,), 0, 1 << 20) % (room + 1)
    tallies = tallies.at[1:1 + 2 * twos:2].set(giver - passed).at[2:2 + 2 * twos:2].set(sink + passed)
    return tallies[jax.random.permutation(jax.random.fold_in(rng, 2), count)]


def deal_out(stream_key, own, number, rows, number_of, top, limit, slope):
    ranking = jax.random.permutation(stream_key, number_of)
    packed, common = load_shares(number_of, rows * top, limit, slope, True), load_shares(number_of, rows * top, limit, slope, False)
    places = jnp.arange(number_of)

    def named(sizes, rotation):
        used = int((sizes > 0).sum())
        fixed = max(1, used // 4)
        moved = fixed + (places - fixed + rotation * (used - fixed)) % max(1, number_of - fixed)
        return jnp.zeros((number_of,), jnp.int32).at[ranking[jnp.where(places < fixed, places, moved)]].set(jnp.asarray(sizes, jnp.int32))

    sizes = jnp.where(number % 4 == 0, named(packed, number // 4), named(common, number - number // 4 - 1))
    mixed = jax.random.permutation(jax.random.fold_in(own, 3), number_of)
    giver, sink = mixed[0:number_of // 2 * 2:2], mixed[1:number_of // 2 * 2:2]
    slack = jnp.minimum(sizes[giver] - 1, limit - sizes[sink]) // 2
    slack = jnp.where((giver == ranking[0]) | (sink == ranking[0]) | (sizes[sink] == 0), 0, jnp.maximum(slack, 0))
    moved = jax.random.randint(jax.random.fold_in(own, 4), (number_of // 2,), 0, 1 << 20) % (slack + 1)
    sizes = sizes.at[giver].add(-moved).at[sink].add(moved)
    members = jnp.searchsorted(jnp.cumsum(sizes), jnp.arange(rows * top), side="right").astype(jnp.int32)
    listing = members.reshape(top, rows).T
    listing = listing[jax.random.permutation(jax.random.fold_in(own, 1), rows)]
    rotation = jax.random.randint(jax.random.fold_in(own, 2), (rows, 1), 0, top)
    return jnp.take_along_axis(listing, (jnp.arange(top)[None, :] + rotation) % top, axis=1)


def load_shares(amount, total, bound, slope, full):
    portions = [(1 << 20) // math.isqrt(rank ** slope) + 1 for rank in range(1, amount + 1)]
    largest = bound if full else min(bound, max(-(-total // amount), total * portions[0] // sum(portions)))
    least = 1 if total - largest >= amount - 1 else 0
    given, spare = [largest] + [least] * (amount - 1), total - largest - least * (amount - 1)
    while spare > 0:
        candidates = [i for i in range(1, amount) if given[i] < largest] or [i for i in range(1, amount) if given[i] < bound]
        whole, left = sum([portions[i] for i in candidates]), spare
        for i in candidates:
            more = min(bound - given[i], max(1, left * portions[i] // whole), spare)
            given[i] = given[i] + more
            spare = spare - more
    return np.array(given)


def gaussian(rng, extent, scale, limit, cuts=(), held_as=jnp.bfloat16):
    array = jax.random.normal(rng, extent, jnp.float32) * scale
    if len(cuts) > 0:
        array = steps_of(rng, extent, cuts, -0.22, 0.18) * array
    return jnp.clip(array, min=-limit, max=limit).astype(held_as)


def setup_inputs(seed: int = 0) -> dict:
    key_of = jax.random.split(jax.random.key(seed), 6)
    query_rows = draw_query_rows(jax.random.fold_in(key_of[5], 71), 0)
    key_rows = draw_key_rows(jax.random.fold_in(key_of[5], 71), 0)
    token_values = gaussian(key_of[2], (TOKEN_ROW_COUNT, KEY_VALUE_HEADS * HEAD_SIZE), 1.0, 6.0, ((0, 256),))
    group_of_row_keys = jax.random.split(jax.random.fold_in(key_of[3], 1), TOKEN_ROW_COUNT // TOK_DEV)
    group_of_row_turns = jax.random.permutation(jax.random.fold_in(key_of[3], 3), TOKEN_ROW_COUNT // TOK_DEV)
    group_of_row = jax.vmap(lambda own, number: deal_out(jax.random.fold_in(key_of[3], 2), own, number, TOK_DEV, GROUPS, 1, SLOT, 2))(group_of_row_keys, group_of_row_turns).reshape((TOKEN_ROW_COUNT, 1))
    doc_lengths = jax.vmap(lambda own: uneven_parts(own, DOCS, GROUP_ROWS, DOC_MOST, 2))(jax.random.split(key_of[4], GROUPS)).reshape((GROUPS, DOCS)).astype(jnp.int32)
    return dict(query_rows=query_rows, key_rows=key_rows, token_values=token_values, group_of_row=group_of_row, doc_lengths=doc_lengths)


masked_score = -1e+30

def reference(query_rows, key_rows, token_values, group_of_row, doc_lengths):
    count_all = query_rows.shape[0]
    group_count = doc_lengths.shape[0]
    rows_per_group = QUERY_HEAD_COUNT // KEY_VALUE_HEADS
    group_ids = group_of_row[:, 0].astype(jnp.int32)
    onehot = (group_ids[:, None] == jnp.arange(group_count, dtype=jnp.int32)[None, :]).astype(jnp.int32)
    ranks = lax.optimization_barrier(jnp.sum((jnp.cumsum(onehot, axis=0) - onehot) * onehot, axis=1))
    lengths = doc_lengths.astype(jnp.int32)
    starts = jnp.cumsum(lengths, axis=1) - lengths
    row_starts = jnp.take(starts, group_ids, axis=0)
    doc_ids = lax.optimization_barrier(jnp.sum((row_starts <= ranks[:, None]).astype(jnp.int32), axis=1)) - 1
    stream = jnp.arange(count_all, dtype=jnp.int32)
    ordering = jnp.argsort(group_ids * count_all + stream).astype(jnp.int32)
    margin = GROUP_ROWS

    def padded(source, filler):
        sorted_rows = jnp.take(source, ordering, axis=0)
        pad_shape = (margin,) + source.shape[1:]
        return jnp.concatenate([jnp.full(pad_shape, filler, source.dtype), sorted_rows], axis=0)
    sorted_queries = jnp.take(query_rows, ordering, axis=0)
    padded_keys = padded(key_rows, 0)
    padded_values = padded(token_values, 0)
    group_pad = padded(group_ids, -1)
    doc_pad = padded(doc_ids, -1)
    index_pad = padded(stream, -1)
    rows_per_block = 128
    causal_window = margin + rows_per_block
    scaling = 1.0 / math.sqrt(HEAD_SIZE)

    def one_block(leading_row):
        block_of_queries = lax.dynamic_slice_in_dim(sorted_queries, leading_row, rows_per_block, 0).astype(jnp.float32).reshape(rows_per_block, KEY_VALUE_HEADS, rows_per_group, HEAD_SIZE)
        block_of_keys = lax.dynamic_slice_in_dim(padded_keys, leading_row, causal_window, 0).astype(jnp.float32).reshape(causal_window, KEY_VALUE_HEADS, HEAD_SIZE)
        block_of_values = lax.dynamic_slice_in_dim(padded_values, leading_row, causal_window, 0).astype(jnp.float32).reshape(causal_window, KEY_VALUE_HEADS, HEAD_SIZE)
        group_keys = lax.dynamic_slice_in_dim(group_pad, leading_row, causal_window, 0)
        doc_keys = lax.dynamic_slice_in_dim(doc_pad, leading_row, causal_window, 0)
        index_keys = lax.dynamic_slice_in_dim(index_pad, leading_row, causal_window, 0)
        group_query = lax.dynamic_slice_in_dim(group_pad, leading_row + margin, rows_per_block, 0)
        doc_query = lax.dynamic_slice_in_dim(doc_pad, leading_row + margin, rows_per_block, 0)
        index_query = lax.dynamic_slice_in_dim(index_pad, leading_row + margin, rows_per_block, 0)
        allowed = (group_query[:, None] == group_keys[None, :]) & (doc_query[:, None] == doc_keys[None, :]) & (index_keys[None, :] <= index_query[:, None])
        scores = jnp.einsum('qjgd,kjd->jgqk', block_of_queries, block_of_keys) * scaling
        scores = jnp.where(allowed[None, None], scores, masked_score)
        row_max = lax.optimization_barrier(jnp.max(scores, axis=3, keepdims=True))
        weights = jnp.exp(scores - row_max)
        totals = lax.optimization_barrier(jnp.sum(weights, axis=3))
        rounded = lax.optimization_barrier(weights.astype(jnp.bfloat16)).astype(jnp.float32)
        output = jnp.einsum('jgqk,kjd->qjgd', rounded, block_of_values)
        output = output / jnp.transpose(totals, (2, 0, 1))[..., None]
        return output.reshape(rows_per_block, QUERY_HEAD_COUNT * HEAD_SIZE).astype(jnp.bfloat16)
    firsts = jnp.arange(count_all // rows_per_block, dtype=jnp.int32) * rows_per_block
    blocks = lax.map(one_block, firsts)
    sorted_out = blocks.reshape(count_all, QUERY_HEAD_COUNT * HEAD_SIZE)
    return jnp.zeros_like(sorted_out).at[ordering].set(sorted_out)
```

```python
import math

import jax
import jax.numpy as jnp
from jax import lax
from jax.experimental import pallas as pl
from jax.experimental.pallas import tpu as pltpu
from jax.sharding import PartitionSpec as P

KV_HEADS = 8
HEAD = 128
PER_KV = 4
GROUPS = 32
SLOT = 8
QW = PER_KV * HEAD
ROW_W = QW + 2 * HEAD
EMPTY = 64.0
FAR = 16384.0
TQ = 256
TK = 256


def slot_targets(group_col):
    rows = group_col.shape[0]
    col = jnp.broadcast_to(group_col.astype(jnp.float32), (rows, rows))
    row = jnp.transpose(col)
    earlier = lax.broadcasted_iota(jnp.int32, (rows, rows), 0) < lax.broadcasted_iota(
        jnp.int32, (rows, rows), 1
    )
    same = jnp.where((col == row) & earlier, 1.0, 0.0)
    position = jnp.sum(same, axis=0, keepdims=True)
    return row[0:1, :] * float(SLOT) + position


def pack_kernel(group_ref, q_ref, k_ref, v_ref, out_ref, pick_ref):
    slots = GROUPS * SLOT
    rows = q_ref.shape[0]

    @pl.when(pl.program_id(0) == 0)
    def _():
        target = slot_targets(group_ref[...])
        slot = lax.broadcasted_iota(jnp.int32, (slots, rows), 0).astype(jnp.float32)
        pick_ref[...] = jnp.where(slot == target, 1.0, 0.0).astype(jnp.bfloat16)

    pick = pick_ref[...]

    def moved(x):
        return jnp.dot(pick, x, preferred_element_type=jnp.float32)

    empty = 1.0 - jnp.sum(pick.astype(jnp.float32), axis=1, keepdims=True)
    v_out = moved(v_ref[...]) + empty * EMPTY
    shape = (GROUPS, 1, SLOT)
    out_ref[:, :, :, 0:QW] = moved(q_ref[...]).astype(jnp.bfloat16).reshape(shape + (QW,))
    out_ref[:, :, :, QW : QW + HEAD] = (
        moved(k_ref[...]).astype(jnp.bfloat16).reshape(shape + (HEAD,))
    )
    out_ref[:, :, :, QW + HEAD :] = v_out.astype(jnp.bfloat16).reshape(shape + (HEAD,))


def pack(group, q, k, v):
    rows = q.shape[0]
    return pl.pallas_call(
        pack_kernel,
        grid=(KV_HEADS,),
        in_specs=[
            pl.BlockSpec((rows, 1), lambda j: (0, 0)),
            pl.BlockSpec((rows, QW), lambda j: (0, j)),
            pl.BlockSpec((rows, HEAD), lambda j: (0, j)),
            pl.BlockSpec((rows, HEAD), lambda j: (0, j)),
        ],
        out_specs=pl.BlockSpec((GROUPS, 1, SLOT, ROW_W), lambda j: (0, j, 0, 0)),
        out_shape=jax.ShapeDtypeStruct((GROUPS, KV_HEADS, SLOT, ROW_W), jnp.bfloat16),
        scratch_shapes=[pltpu.VMEM((GROUPS * SLOT, rows), jnp.bfloat16)],
        name="pack",
    )(group, q, k, v)


def unpack_kernel(group_ref, o_ref, out_ref, pick_ref):
    slots = GROUPS * SLOT
    rows = out_ref.shape[0]

    @pl.when(pl.program_id(0) == 0)
    def _():
        target = slot_targets(group_ref[...])
        slot = lax.broadcasted_iota(jnp.int32, (slots, rows), 0).astype(jnp.float32)
        pick_ref[...] = jnp.transpose(jnp.where(slot == target, 1.0, 0.0)).astype(jnp.bfloat16)

    x = o_ref[...].reshape(slots, QW)
    out_ref[...] = jnp.dot(pick_ref[...], x, preferred_element_type=jnp.float32).astype(
        jnp.bfloat16
    )


def unpack(group, o):
    rows = group.shape[0]
    return pl.pallas_call(
        unpack_kernel,
        grid=(KV_HEADS,),
        in_specs=[
            pl.BlockSpec((rows, 1), lambda j: (0, 0)),
            pl.BlockSpec((GROUPS, 1, SLOT, QW), lambda j: (0, j, 0, 0)),
        ],
        out_specs=pl.BlockSpec((rows, QW), lambda j: (0, j)),
        out_shape=jax.ShapeDtypeStruct((rows, KV_HEADS * QW), jnp.bfloat16),
        scratch_shapes=[pltpu.VMEM((rows, GROUPS * SLOT), jnp.bfloat16)],
        name="unpack",
    )(group, o)


def attend_kernel(len_ref, q_ref, k_ref, v_ref, o_ref, key_ref, mask_ref, first_ref):
    count = k_ref.shape[0]
    block = pl.program_id(0)
    chunk = 128

    @pl.when(block == 0)
    def _():
        first_len = len_ref[0, 0].astype(jnp.float32)
        lower = jnp.where(
            lax.broadcasted_iota(jnp.int32, (chunk, chunk), 0)
            > lax.broadcasted_iota(jnp.int32, (chunk, chunk), 1),
            1.0,
            0.0,
        ).astype(jnp.bfloat16)
        lane = lax.broadcasted_iota(jnp.int32, (chunk, chunk), 1).astype(jnp.float32)
        row = lax.broadcasted_iota(jnp.int32, (chunk, chunk), 0).astype(jnp.float32)

        def one(i, carry):
            seen, first = carry
            at = pl.ds(pl.multiple_of(i * chunk, chunk), chunk)
            head = v_ref[at, :].astype(jnp.float32)[:, 0:1]
            used = jnp.broadcast_to(jnp.where(head < 0.5 * EMPTY, 1.0, 0.0), (chunk, chunk))
            rank = seen + jnp.dot(
                lower, used.astype(jnp.bfloat16), preferred_element_type=jnp.float32
            )
            code = jnp.where(used > 0.5, jnp.where(rank < first_len, 0.0, 1.0), 2.0)
            key_ref[at, 0:chunk] = k_ref[at, :]
            key_ref[at, chunk:] = jnp.where(lane == code, 1.0, 0.0).astype(jnp.bfloat16)
            mask_ref[at, :] = jnp.where(
                (lane < 2.5) & (lane != code), -FAR, 0.0
            ).astype(jnp.bfloat16)
            place = jnp.where(code == 1.0, row + (i * chunk).astype(jnp.float32), float(count))
            seen = seen + jnp.sum(used, axis=0, keepdims=True)
            return seen, jnp.minimum(first, jnp.min(place, axis=0, keepdims=True))

        start = (jnp.zeros((1, chunk), jnp.float32), jnp.full((1, chunk), float(count)))
        _, first = lax.fori_loop(0, count // chunk, one, start)
        first_ref[0] = jnp.min(first).astype(jnp.int32)

    first = first_ref[0]
    q_start = block * TQ
    scale = 1.0 / math.sqrt(HEAD)
    mask = mask_ref[pl.ds(pl.multiple_of(q_start, TQ), TQ), :]
    q = jnp.concatenate(
        [
            jnp.concatenate([q_ref[:, h * HEAD : (h + 1) * HEAD], mask], axis=1)
            for h in range(PER_KV)
        ],
        axis=0,
    )

    def step(b, carry, diagonal):
        m, total, acc = carry
        at = pl.ds(pl.multiple_of(b * TK, TK), TK)
        s = lax.dot_general(
            q, key_ref[at, :], (((1,), (1,)), ((), ())), preferred_element_type=jnp.float32
        )
        if diagonal:
            t = lax.broadcasted_iota(jnp.int32, (TQ, TK), 0)
            u = lax.broadcasted_iota(jnp.int32, (TQ, TK), 1)
            bias = jnp.where(u <= t, 0.0, -2.0 * FAR)
            s = (s.reshape(PER_KV, TQ, TK) + bias[None]).reshape(PER_KV * TQ, TK)
        m_new = jnp.maximum(m, jnp.max(s, axis=1, keepdims=True))
        w = jnp.exp((s - m_new) * scale)
        fade = jnp.exp((m - m_new) * scale)
        total = total * fade + jnp.sum(w, axis=1, keepdims=True)
        acc = acc * fade + jnp.dot(
            w.astype(jnp.bfloat16), v_ref[at, :], preferred_element_type=jnp.float32
        )
        return m_new, total, acc

    lowest = jnp.where(q_start >= first, first // TK, 0)
    rows = PER_KV * TQ
    carry = (
        jnp.full((rows, 1), -4.0 * FAR, jnp.float32),
        jnp.zeros((rows, 1), jnp.float32),
        jnp.zeros((rows, HEAD), jnp.float32),
    )
    carry = lax.fori_loop(lowest, block, lambda b, c: step(b, c, False), carry)
    _, total, acc = step(block, carry, True)
    out = (acc / total).astype(jnp.bfloat16)
    for h in range(PER_KV):
        o_ref[:, h * HEAD : (h + 1) * HEAD] = out[h * TQ : (h + 1) * TQ, :]


def attend(lengths, rows):
    count = rows.shape[0]
    return pl.pallas_call(
        attend_kernel,
        grid=(count // TQ,),
        in_specs=[
            pl.BlockSpec(memory_space=pltpu.SMEM),
            pl.BlockSpec((TQ, QW), lambda i: (i, 0)),
            pl.BlockSpec((count, HEAD), lambda i: (0, PER_KV)),
            pl.BlockSpec((count, HEAD), lambda i: (0, PER_KV + 1)),
        ],
        out_specs=pl.BlockSpec((TQ, QW), lambda i: (i, 0)),
        out_shape=jax.ShapeDtypeStruct((count, QW), jnp.bfloat16),
        scratch_shapes=[
            pltpu.VMEM((count, 2 * HEAD), jnp.bfloat16),
            pltpu.VMEM((count, HEAD), jnp.bfloat16),
            pltpu.SMEM((1,), jnp.int32),
        ],
        name="attend",
    )(lengths, rows, rows, rows)


def body(query_rows, key_rows, token_values, group_of_row, doc_lengths):
    devices = lax.axis_size("dp") * lax.axis_size("ctx")
    packed = pack(group_of_row, query_rows, key_rows, token_values)
    arrived = lax.all_to_all(
        packed.reshape(devices, SLOT, ROW_W), ("dp", "ctx"), split_axis=0, concat_axis=0, tiled=True
    )
    result = attend(doc_lengths, arrived.reshape(devices * SLOT, ROW_W))
    returned = lax.all_to_all(
        result.reshape(devices, SLOT, QW), ("dp", "ctx"), split_axis=0, concat_axis=0, tiled=True
    )
    return unpack(group_of_row, returned.reshape(GROUPS, KV_HEADS, SLOT, QW))


def solution(mesh):
    rows = P(("dp", "ctx"), None)
    return jax.shard_map(
        body,
        mesh=mesh,
        in_specs=(rows, rows, rows, rows, P("dp", None)),
        out_specs=rows,
        check_vma=False,
    )
```

```python
import functools
import math

import jax
import jax.numpy as jnp
from jax import lax
from jax.experimental import pallas as pl
from jax.experimental.pallas import tpu as pltpu
from jax.sharding import PartitionSpec as P

KV_HEADS = 8
HEAD = 128
PER_KV = 4
GROUPS = 32
SLOT = 8
QW = PER_KV * HEAD
HALF = QW // 2
EMPTY = 64.0
FAR = 16384.0
TQ = 256
TK = 256
VALUE_ROWS = HEAD + 16


def slot_targets(group_col):
    rows = group_col.shape[0]
    col = jnp.broadcast_to(group_col.astype(jnp.float32), (rows, rows))
    row = jnp.transpose(col)
    earlier = lax.broadcasted_iota(jnp.int32, (rows, rows), 0) < lax.broadcasted_iota(
        jnp.int32, (rows, rows), 1
    )
    same = jnp.where((col == row) & earlier, 1.0, 0.0)
    position = jnp.sum(same, axis=0, keepdims=True)
    return row[0:1, :] * float(SLOT) + position


def pack_kernel(group_ref, q_ref, k_ref, v_ref, near_ref, far_ref, pick_ref):
    slots = GROUPS * SLOT
    rows = q_ref.shape[0]

    @pl.when(pl.program_id(0) == 0)
    def _():
        target = slot_targets(group_ref[...])
        slot = lax.broadcasted_iota(jnp.int32, (slots, rows), 0).astype(jnp.float32)
        pick_ref[...] = jnp.where(slot == target, 1.0, 0.0).astype(jnp.bfloat16)

    pick = pick_ref[...]

    def moved(x):
        return jnp.dot(pick, x, preferred_element_type=jnp.float32)

    def laid(x):
        return x.reshape(GROUPS, 1, SLOT, x.shape[1]).astype(jnp.bfloat16)

    empty = 1.0 - jnp.sum(pick.astype(jnp.float32), axis=1, keepdims=True)
    near_ref[:, :, :, 0:HALF] = laid(moved(q_ref[:, 0:HALF]))
    near_ref[:, :, :, HALF : HALF + HEAD] = laid(moved(k_ref[...]))
    near_ref[:, :, :, HALF + HEAD :] = laid(moved(v_ref[...]) + empty * EMPTY)
    far_ref[...] = laid(moved(q_ref[:, HALF:]))


def pack(group, q, k, v):
    rows = q.shape[0]
    widths = (HALF + 2 * HEAD, HALF)
    return pl.pallas_call(
        pack_kernel,
        grid=(KV_HEADS,),
        in_specs=[
            pl.BlockSpec((rows, 1), lambda j: (0, 0)),
            pl.BlockSpec((rows, QW), lambda j: (0, j)),
            pl.BlockSpec((rows, HEAD), lambda j: (0, j)),
            pl.BlockSpec((rows, HEAD), lambda j: (0, j)),
        ],
        out_specs=[
            pl.BlockSpec((GROUPS, 1, SLOT, w), lambda j: (0, j, 0, 0)) for w in widths
        ],
        out_shape=[
            jax.ShapeDtypeStruct((GROUPS, KV_HEADS, SLOT, w), jnp.bfloat16) for w in widths
        ],
        scratch_shapes=[pltpu.VMEM((GROUPS * SLOT, rows), jnp.bfloat16)],
        name="pack",
    )(group, q, k, v)


def unpack_kernel(group_ref, near_ref, far_ref, out_ref, pick_ref):
    slots = GROUPS * SLOT
    rows = out_ref.shape[0]

    @pl.when(pl.program_id(0) == 0)
    def _():
        target = slot_targets(group_ref[...])
        slot = lax.broadcasted_iota(jnp.int32, (slots, rows), 0).astype(jnp.float32)
        pick_ref[...] = jnp.transpose(jnp.where(slot == target, 1.0, 0.0)).astype(jnp.bfloat16)

    for part, ref in enumerate((near_ref, far_ref)):
        out_ref[:, part * HALF : (part + 1) * HALF] = jnp.dot(
            pick_ref[...], ref[...].reshape(slots, HALF), preferred_element_type=jnp.float32
        ).astype(jnp.bfloat16)


def unpack(group, near, far):
    rows = group.shape[0]
    part = pl.BlockSpec((GROUPS, 1, SLOT, HALF), lambda j: (0, j, 0, 0))
    return pl.pallas_call(
        unpack_kernel,
        grid=(KV_HEADS,),
        in_specs=[pl.BlockSpec((rows, 1), lambda j: (0, 0)), part, part],
        out_specs=pl.BlockSpec((rows, QW), lambda j: (0, j)),
        out_shape=jax.ShapeDtypeStruct((rows, KV_HEADS * QW), jnp.bfloat16),
        scratch_shapes=[pltpu.VMEM((rows, GROUPS * SLOT), jnp.bfloat16)],
        name="unpack",
    )(group, near, far)


def attend_kernel(heads, len_ref, q_ref, k_ref, v_ref, o_ref, key_ref, vt_ref, mask_ref, acc_ref, first_ref):
    count = k_ref.shape[0]
    block = pl.program_id(0)
    chunk = 128

    @pl.when(block == 0)
    def _():
        first_len = len_ref[0, 0].astype(jnp.float32)
        r = lax.broadcasted_iota(jnp.int32, (chunk, chunk), 0)
        l = lax.broadcasted_iota(jnp.int32, (chunk, chunk), 1)
        lower = jnp.where(r > l, 1.0, 0.0).astype(jnp.bfloat16)
        lane = l.astype(jnp.float32)
        row = r.astype(jnp.float32)
        seen = jnp.zeros((1, chunk), jnp.float32)
        first = jnp.full((1, chunk), float(count))
        ones = jnp.where(lax.broadcasted_iota(jnp.int32, (VALUE_ROWS - HEAD, chunk), 0) == 0, 1.0, 0.0).astype(jnp.bfloat16)
        for i in range(count // chunk):
            at = pl.ds(i * chunk, chunk)
            v = v_ref[at, :]
            vf = v.astype(jnp.float32)
            used = jnp.broadcast_to(jnp.where(vf[:, 0:1] < 0.5 * EMPTY, 1.0, 0.0), (chunk, chunk))
            rank = seen + jnp.dot(lower, used.astype(jnp.bfloat16), preferred_element_type=jnp.float32)
            code = jnp.where(used > 0.5, jnp.where(rank < first_len, 0.0, 1.0), 2.0)
            key_ref[at, 0:chunk] = k_ref[at, :]
            key_ref[at, chunk:] = jnp.where(lane == code, 1.0, 0.0).astype(jnp.bfloat16)
            mask_ref[at, :] = jnp.where((lane < 2.5) & (lane != code), -FAR, 0.0).astype(jnp.bfloat16)
            vt_ref[0:HEAD, at] = jnp.transpose(vf).astype(jnp.bfloat16)
            vt_ref[HEAD:, at] = ones
            place = jnp.where(code == 1.0, row + float(i * chunk), float(count))
            seen = seen + jnp.sum(used, axis=0, keepdims=True)
            first = jnp.minimum(first, jnp.min(place, axis=0, keepdims=True))
        first_ref[0] = jnp.min(first).astype(jnp.int32)
    first = first_ref[0]
    q_start = block * TQ
    scale = math.log2(math.e) / math.sqrt(HEAD)
    mask = mask_ref[pl.ds(pl.multiple_of(q_start, TQ), TQ), :]
    qs = [jnp.concatenate([q_ref[:, h*HEAD:(h+1)*HEAD], mask], axis=1) for h in range(heads)]
    def step(b, ms, kind):
        at = pl.ds(pl.multiple_of(b * TK, TK), TK)
        key = key_ref[at, :]
        vt = vt_ref[:, at]
        new = []
        if kind == "diag":
            t = q_start + lax.broadcasted_iota(jnp.int32, (TK, TQ), 1)
            u = b * TK + lax.broadcasted_iota(jnp.int32, (TK, TQ), 0)
            bias = jnp.where(u <= t, 0.0, -2.0 * FAR)
        for h in range(heads):
            s = lax.dot_general(key, qs[h], (((1,), (1,)), ((), ())), preferred_element_type=jnp.float32)
            if kind == "diag":
                s = s + bias
            m_new = jnp.maximum(ms[h], jnp.max(s, axis=0, keepdims=True))
            w = jnp.exp2((s - m_new) * scale).astype(jnp.bfloat16)
            fade = jnp.exp2((ms[h] - m_new) * scale)
            acc_ref[h] = acc_ref[h] * fade + jnp.dot(vt, w, preferred_element_type=jnp.float32)
            new.append(m_new)
        return tuple(new)
    acc_ref[...] = jnp.zeros_like(acc_ref)
    lowest = jnp.where(q_start >= first, first // TK, 0)
    last = (q_start + TQ - 1) // TK
    ms = tuple(jnp.full((1, TQ), -4.0 * FAR, jnp.float32) for _ in range(heads))
    full = q_start // TK
    ms = lax.fori_loop(lowest, full, lambda b, c: step(b, c, "full"), ms)
    ndiag = max(TQ // TK, 1)
    for d in range(ndiag):
        ms = step(full + d, ms, "diag")
    for h in range(heads):
        acc = acc_ref[h]
        o = acc[0:HEAD] * (1.0 / acc[HEAD:HEAD+1])
        o_ref[:, h*HEAD:(h+1)*HEAD] = jnp.transpose(o).astype(jnp.bfloat16)
def attend(lengths, q, kv):
    count, width = q.shape
    used = kv.shape[1] // HEAD
    heads = PER_KV // 2
    return pl.pallas_call(
        functools.partial(attend_kernel, heads),
        grid=(count // TQ,),
        in_specs=[
            pl.BlockSpec(memory_space=pltpu.SMEM),
            pl.BlockSpec((TQ, heads * HEAD), lambda i: (i, 0)),
            pl.BlockSpec((count, HEAD), lambda i: (0, used - 2)),
            pl.BlockSpec((count, HEAD), lambda i: (0, used - 1)),
        ],
        out_specs=pl.BlockSpec((TQ, heads * HEAD), lambda i: (i, 0)),
        out_shape=jax.ShapeDtypeStruct((count, heads * HEAD), jnp.bfloat16),
        scratch_shapes=[
            pltpu.VMEM((count, 2 * HEAD), jnp.bfloat16),
            pltpu.VMEM((VALUE_ROWS, count), jnp.bfloat16),
            pltpu.VMEM((count, HEAD), jnp.bfloat16),
            pltpu.VMEM((heads, VALUE_ROWS, TQ), jnp.float32),
            pltpu.SMEM((1,), jnp.int32),
        ],
        cost_estimate=pl.CostEstimate(
            flops=2 * heads * count * count * HEAD, transcendentals=heads * count * count // 2, bytes_accessed=6 * count * width
        ),
        name="attend",
    )(lengths, q, kv, kv)


def exchange(x):
    devices = lax.axis_size("dp") * lax.axis_size("ctx")
    return lax.all_to_all(
        x.reshape(devices, SLOT, x.shape[-1]), ("dp", "ctx"), split_axis=0, concat_axis=0, tiled=True
    )


def body(query_rows, key_rows, token_values, group_of_row, doc_lengths):
    def flat(x):
        return x.reshape(x.shape[0] * SLOT, x.shape[-1])

    def home(x):
        return exchange(x).reshape(GROUPS, KV_HEADS, SLOT, HALF)

    near, far = pack(group_of_row, query_rows, key_rows, token_values)
    near, far = lax.optimization_barrier((exchange(near), far))
    near = flat(near)
    far = flat(exchange(far))
    near_out = home(attend(doc_lengths, near, near))
    far_out = home(attend(doc_lengths, far, near))
    return unpack(group_of_row, near_out, far_out)


def solution(mesh):
    rows = P(("dp", "ctx"), None)
    return jax.shard_map(
        body,
        mesh=mesh,
        in_specs=(rows, rows, rows, rows, P("dp", None)),
        out_specs=rows,
        check_vma=False,
    )
```

```python
import math

import jax
import jax.numpy as jnp
from jax import lax
from jax.experimental import pallas as pl
from jax.experimental.pallas import tpu as pltpu
from jax.sharding import PartitionSpec as P

KV_HEADS = 8
HEAD = 128
PER_KV = 4
GROUPS = 32
SLOT = 8
QW = PER_KV * HEAD
ROW_W = QW + 2 * HEAD
EMPTY = 64.0
FAR = 16384.0
TQ = 256
TK = 512
VALUE_ROWS = HEAD + 16
STEP = 2


def slot_targets(group_row):
    rows = group_row.shape[1]
    row = jnp.broadcast_to(group_row.astype(jnp.float32), (rows, rows))
    col = jnp.transpose(row)
    earlier = lax.broadcasted_iota(jnp.int32, (rows, rows), 0) < lax.broadcasted_iota(
        jnp.int32, (rows, rows), 1
    )
    same = jnp.where((col == row) & earlier, 1.0, 0.0)
    position = jnp.sum(same, axis=0, keepdims=True)
    return row[0:1, :] * float(SLOT) + position


def pack_kernel(group_ref, q_ref, k_ref, v_ref, out_ref, pick_ref):
    slots = GROUPS * SLOT
    rows = q_ref.shape[0]

    @pl.when(pl.program_id(0) == 0)
    def _():
        target = slot_targets(group_ref[...])
        slot = lax.broadcasted_iota(jnp.int32, (slots, rows), 0).astype(jnp.float32)
        pick_ref[...] = jnp.where(slot == target, 1.0, 0.0).astype(jnp.bfloat16)

    pick = pick_ref[...]

    def moved(x):
        return jnp.dot(pick, x, preferred_element_type=jnp.float32)

    def laid(x):
        return x.reshape(GROUPS, SLOT, x.shape[1]).astype(jnp.bfloat16)

    empty = (1.0 - jnp.sum(pick.astype(jnp.float32), axis=1, keepdims=True)) * EMPTY
    for j in range(STEP):
        head = slice(j * HEAD, (j + 1) * HEAD)
        out_ref[:, j, :, 0:QW] = laid(moved(q_ref[:, j * QW : (j + 1) * QW]))
        out_ref[:, j, :, QW : QW + HEAD] = laid(moved(k_ref[:, head]))
        out_ref[:, j, :, QW + HEAD :] = laid(moved(v_ref[:, head]) + empty)


def pack(group, q, k, v):
    rows = q.shape[0]
    return pl.pallas_call(
        pack_kernel,
        grid=(KV_HEADS // STEP,),
        in_specs=[
            pl.BlockSpec((1, rows), lambda j: (0, 0)),
            pl.BlockSpec((rows, STEP * QW), lambda j: (0, j)),
            pl.BlockSpec((rows, STEP * HEAD), lambda j: (0, j)),
            pl.BlockSpec((rows, STEP * HEAD), lambda j: (0, j)),
        ],
        out_specs=pl.BlockSpec((GROUPS, STEP, SLOT, ROW_W), lambda j: (0, j, 0, 0)),
        out_shape=jax.ShapeDtypeStruct((GROUPS, KV_HEADS, SLOT, ROW_W), jnp.bfloat16),
        scratch_shapes=[pltpu.VMEM((GROUPS * SLOT, rows), jnp.bfloat16)],
        name="pack",
    )(group, q, k, v)


def unpack_kernel(group_ref, o_ref, out_ref, pick_ref):
    slots = GROUPS * SLOT
    rows = out_ref.shape[0]

    @pl.when(pl.program_id(0) == 0)
    def _():
        target = slot_targets(group_ref[...])
        slot = lax.broadcasted_iota(jnp.int32, (slots, rows), 0).astype(jnp.float32)
        pick_ref[...] = jnp.transpose(jnp.where(slot == target, 1.0, 0.0)).astype(jnp.bfloat16)

    for j in range(STEP):
        x = o_ref[:, j].reshape(slots, QW)
        out_ref[:, j * QW : (j + 1) * QW] = jnp.dot(
            pick_ref[...], x, preferred_element_type=jnp.float32
        ).astype(jnp.bfloat16)


def unpack(group, o):
    rows = group.shape[1]
    return pl.pallas_call(
        unpack_kernel,
        grid=(KV_HEADS // STEP,),
        in_specs=[
            pl.BlockSpec((1, rows), lambda j: (0, 0)),
            pl.BlockSpec((GROUPS, STEP, SLOT, QW), lambda j: (0, j, 0, 0)),
        ],
        out_specs=pl.BlockSpec((rows, STEP * QW), lambda j: (0, j)),
        out_shape=jax.ShapeDtypeStruct((rows, KV_HEADS * QW), jnp.bfloat16),
        scratch_shapes=[pltpu.VMEM((rows, GROUPS * SLOT), jnp.bfloat16)],
        name="unpack",
    )(group, o)


def attend_kernel(len_ref, q_ref, k_ref, v_ref, o_ref, key_ref, vt_ref, mask_ref, acc_ref, s_ref, first_ref):
    count = k_ref.shape[0]
    block = pl.program_id(0)
    chunk = 128
    heads = PER_KV

    @pl.when(block == 0)
    def _():
        first_len = len_ref[0, 0].astype(jnp.float32)
        r = lax.broadcasted_iota(jnp.int32, (chunk, chunk), 0)
        l = lax.broadcasted_iota(jnp.int32, (chunk, chunk), 1)
        lower = jnp.where(r > l, 1.0, 0.0).astype(jnp.bfloat16)
        lane = l.astype(jnp.float32)
        row = r.astype(jnp.float32)
        seen = jnp.zeros((1, chunk), jnp.float32)
        first = jnp.full((1, chunk), float(count))
        ones = jnp.where(lax.broadcasted_iota(jnp.int32, (VALUE_ROWS - HEAD, chunk), 0) == 0, 1.0, 0.0).astype(jnp.bfloat16)
        for i in range(count // chunk):
            at = pl.ds(i * chunk, chunk)
            v = v_ref[at, :]
            vf = v.astype(jnp.float32)
            used = jnp.broadcast_to(jnp.where(vf[:, 0:1] < 0.5 * EMPTY, 1.0, 0.0), (chunk, chunk))
            rank = seen + jnp.dot(lower, used.astype(jnp.bfloat16), preferred_element_type=jnp.float32)
            code = jnp.where(used > 0.5, jnp.where(rank < first_len, 0.0, 1.0), 2.0)
            key_ref[at, 0:chunk] = k_ref[at, :]
            key_ref[at, chunk:] = jnp.where(lane == code, 1.0, 0.0).astype(jnp.bfloat16)
            mask_ref[at, :] = jnp.where((lane < 2.5) & (lane != code), -FAR, 0.0).astype(jnp.bfloat16)
            vt_ref[0:HEAD, at] = jnp.transpose(vf).astype(jnp.bfloat16)
            vt_ref[HEAD:, at] = ones
            place = jnp.where(code == 1.0, row + float(i * chunk), float(count))
            seen = seen + jnp.sum(used, axis=0, keepdims=True)
            first = jnp.minimum(first, jnp.min(place, axis=0, keepdims=True))
        first_ref[0] = jnp.min(first).astype(jnp.int32)
    first = first_ref[0]
    q_start = block * TQ
    scale = math.log2(math.e) / math.sqrt(HEAD)
    mask = mask_ref[pl.ds(pl.multiple_of(q_start, TQ), TQ), :]
    qs = [jnp.concatenate([q_ref[:, h*HEAD:(h+1)*HEAD], mask], axis=1) for h in range(heads)]
    def step(b, ms, kind):
        at = pl.ds(pl.multiple_of(b * TK, TK), TK)
        key = key_ref[at, :]
        vt = vt_ref[:, at]
        new = []
        if kind == "diag":
            t = q_start + lax.broadcasted_iota(jnp.int32, (TK, TQ), 1)
            u = b * TK + lax.broadcasted_iota(jnp.int32, (TK, TQ), 0)
            bias = jnp.where(u <= t, 0.0, -2.0 * FAR)
        for h in range(heads):
            s_ref[h] = lax.dot_general(key, qs[h], (((1,), (1,)), ((), ())), preferred_element_type=jnp.float32)
        for h in range(heads):
            s = s_ref[h]
            if kind == "diag":
                s = s + bias
            m_new = jnp.maximum(ms[h], jnp.max(s, axis=0, keepdims=True))
            w = jnp.exp2((s - m_new) * scale).astype(jnp.bfloat16)
            fade = jnp.exp2((ms[h] - m_new) * scale)
            acc_ref[h] = acc_ref[h] * fade + jnp.dot(vt, w, preferred_element_type=jnp.float32)
            new.append(m_new)
        return tuple(new)
    acc_ref[...] = jnp.zeros_like(acc_ref)
    lowest = jnp.where(q_start >= first, first // TK, 0)
    last = (q_start + TQ - 1) // TK
    ms = tuple(jnp.full((1, TQ), -4.0 * FAR, jnp.float32) for _ in range(heads))
    full = q_start // TK
    ms = lax.fori_loop(lowest, full, lambda b, c: step(b, c, "full"), ms)
    ndiag = max(TQ // TK, 1)
    for d in range(ndiag):
        ms = step(full + d, ms, "diag")
    for h in range(heads):
        acc = acc_ref[h]
        o = acc[0:HEAD] * (1.0 / acc[HEAD:HEAD+1])
        o_ref[:, h*HEAD:(h+1)*HEAD] = jnp.transpose(o).astype(jnp.bfloat16)


def attend(lengths, rows):
    count = rows.shape[0]
    return pl.pallas_call(
        attend_kernel,
        grid=(count // TQ,),
        in_specs=[
            pl.BlockSpec(memory_space=pltpu.SMEM),
            pl.BlockSpec((TQ, QW), lambda i: (i, 0)),
            pl.BlockSpec((count, HEAD), lambda i: (0, PER_KV)),
            pl.BlockSpec((count, HEAD), lambda i: (0, PER_KV + 1)),
        ],
        out_specs=pl.BlockSpec((TQ, QW), lambda i: (i, 0)),
        out_shape=jax.ShapeDtypeStruct((count, QW), jnp.bfloat16),
        scratch_shapes=[
            pltpu.VMEM((count, 2 * HEAD), jnp.bfloat16),
            pltpu.VMEM((VALUE_ROWS, count), jnp.bfloat16),
            pltpu.VMEM((count, HEAD), jnp.bfloat16),
            pltpu.VMEM((PER_KV, VALUE_ROWS, TQ), jnp.float32),
            pltpu.VMEM((PER_KV, TK, TQ), jnp.float32),
            pltpu.SMEM((1,), jnp.int32),
        ],
        name="attend",
    )(lengths, rows, rows, rows)


def body(query_rows, key_rows, token_values, group_of_row, doc_lengths):
    devices = lax.axis_size("dp") * lax.axis_size("ctx")
    group = group_of_row.reshape(1, group_of_row.shape[0])
    packed = pack(group, query_rows, key_rows, token_values)
    arrived = lax.all_to_all(
        packed.reshape(devices, SLOT, ROW_W), ("dp", "ctx"), split_axis=0, concat_axis=0, tiled=True
    )
    result = attend(doc_lengths, arrived.reshape(devices * SLOT, ROW_W))
    returned = lax.all_to_all(
        result.reshape(devices, SLOT, QW), ("dp", "ctx"), split_axis=0, concat_axis=0, tiled=True
    )
    return unpack(group, returned.reshape(GROUPS, KV_HEADS, SLOT, QW))


def solution(mesh):
    rows = P(("dp", "ctx"), None)
    return jax.shard_map(
        body,
        mesh=mesh,
        in_specs=(rows, rows, rows, rows, P("dp", None)),
        out_specs=rows,
        check_vma=False,
    )
```

```python
import math

import jax
import jax.numpy as jnp
from jax import lax
from jax.experimental import pallas as pl
from jax.experimental.pallas import tpu as pltpu
from jax.sharding import PartitionSpec as P

KV_HEADS = 8
HEAD = 128
PER_KV = 4
GROUPS = 32
SLOT = 8
CTX = 8
QW = PER_KV * HEAD
EMPTY = 64.0
FAR = 16384.0
SPAN = 8
BLOCKS = GROUPS // SPAN
KEYS = CTX * SPAN * SLOT
ROWS = SPAN * SLOT
LANES = PER_KV * ROWS
VALUE_ROWS = HEAD + 16
PARTS = 2
HEADS = KV_HEADS // PARTS


def slot_targets(group_row):
    rows = group_row.shape[1]
    row = jnp.broadcast_to(group_row.astype(jnp.float32), (rows, rows))
    col = jnp.transpose(row)
    earlier = lax.broadcasted_iota(jnp.int32, (rows, rows), 0) < lax.broadcasted_iota(
        jnp.int32, (rows, rows), 1
    )
    same = jnp.where((col == row) & earlier, 1.0, 0.0)
    position = jnp.sum(same, axis=0, keepdims=True)
    return row[0:1, :] * float(SLOT) + position


def selection(group_row):
    slots, rows = GROUPS * SLOT, group_row.shape[1]
    slot = lax.broadcasted_iota(jnp.int32, (slots, rows), 0).astype(jnp.float32)
    return jnp.where(slot == slot_targets(group_row), 1.0, 0.0)


def laid(x):
    return x.reshape(GROUPS, SLOT, x.shape[1]).astype(jnp.bfloat16)


def pack_kv_kernel(group_ref, k_ref, v_ref, out_ref):
    pick = selection(group_ref[...])
    empty = (1.0 - jnp.sum(pick, axis=1, keepdims=True)) * EMPTY
    pick = pick.astype(jnp.bfloat16)
    width = k_ref.shape[1]
    out_ref[:, :, 0:width] = laid(jnp.dot(pick, k_ref[...], preferred_element_type=jnp.float32))
    out_ref[:, :, width:] = laid(
        jnp.dot(pick, v_ref[...], preferred_element_type=jnp.float32) + empty
    )


def pack_kv(group, k, v):
    return pl.pallas_call(
        pack_kv_kernel,
        out_shape=jax.ShapeDtypeStruct((GROUPS, SLOT, 2 * k.shape[1]), jnp.bfloat16),
        name="pack_kv",
    )(group, k, v)


def pack_q_kernel(group_ref, q_ref, *refs):
    outs, pick_ref = refs[:-1], refs[-1]
    step = pl.program_id(0)

    @pl.when(step == 0)
    def _():
        pick_ref[...] = selection(group_ref[...]).astype(jnp.bfloat16)

    for part, out_ref in enumerate(outs):

        @pl.when(step == part)
        def _(out_ref=out_ref):
            out_ref[...] = laid(
                jnp.dot(pick_ref[...], q_ref[...], preferred_element_type=jnp.float32)
            )


def pack_q(group, q):
    rows, width = q.shape
    part = width // PARTS
    shape = (GROUPS, SLOT, part)
    return pl.pallas_call(
        pack_q_kernel,
        grid=(PARTS,),
        in_specs=[
            pl.BlockSpec((1, rows), lambda i: (0, 0)),
            pl.BlockSpec((rows, part), lambda i: (0, i)),
        ],
        out_specs=[pl.BlockSpec(shape, lambda i: (0, 0, 0))] * PARTS,
        out_shape=[jax.ShapeDtypeStruct(shape, jnp.bfloat16)] * PARTS,
        scratch_shapes=[pltpu.VMEM((GROUPS * SLOT, rows), jnp.bfloat16)],
        name="pack_q",
    )(group, q)


def unpack_kernel(group_ref, *refs):
    parts, out_ref = refs[:-1], refs[-1]
    pick = jnp.transpose(selection(group_ref[...])).astype(jnp.bfloat16)
    for i, ref in enumerate(parts):
        width = ref.shape[2]
        out_ref[:, i * width : (i + 1) * width] = jnp.dot(
            pick, ref[...].reshape(GROUPS * SLOT, width), preferred_element_type=jnp.float32
        ).astype(jnp.bfloat16)


def unpack(group, parts):
    return pl.pallas_call(
        unpack_kernel,
        out_shape=jax.ShapeDtypeStruct(
            (group.shape[1], sum(p.shape[2] for p in parts)), jnp.bfloat16
        ),
        name="unpack",
    )(group, *parts)


def attend_kernel(
    len_ref, me_ref, q_ref, k_ref, v_ref, o_ref, feat_ref, mask_ref, bias_ref, vt_ref, s_ref
):
    @pl.when(pl.program_id(0) == 0)
    def _():
        me = me_ref[0, 0]
        first_len = len_ref[0, 0].astype(jnp.float32)
        shape = (GROUPS, SLOT, HEAD)
        lane = lax.broadcasted_iota(jnp.int32, shape, 2).astype(jnp.float32)
        slot = lax.broadcasted_iota(jnp.int32, shape, 1).astype(jnp.float32)
        used = [
            jnp.broadcast_to(
                jnp.where(v_ref[c].astype(jnp.float32)[:, :, 0:1] < 0.5 * EMPTY, 1.0, 0.0), shape
            )
            for c in range(CTX)
        ]
        number = [jnp.sum(u, axis=1) for u in used]
        before = jnp.where(
            lax.broadcasted_iota(jnp.int32, (GROUPS, GROUPS), 0)
            > lax.broadcasted_iota(jnp.int32, (GROUPS, GROUPS), 1),
            1.0,
            0.0,
        )
        base = jnp.dot(
            before.astype(jnp.bfloat16),
            sum(number).astype(jnp.bfloat16),
            preferred_element_type=jnp.float32,
        )
        own = jnp.zeros(shape, jnp.float32)
        for c in range(CTX):
            rank = base[:, None, :] + slot
            base = base + number[c]
            code = jnp.where(used[c] > 0.5, jnp.where(rank < first_len, 0.0, 1.0), 2.0)
            own = own + jnp.where(me == c, code, 0.0)
            feat = jnp.where(lane == code, 1.0, 0.0)
            for b in range(BLOCKS):
                feat_ref[b, c * ROWS : (c + 1) * ROWS, :] = (
                    feat[b * SPAN : (b + 1) * SPAN].reshape(ROWS, HEAD).astype(jnp.bfloat16)
                )
        mask_ref[...] = (
            jnp.where(lane == own, 0.0, -FAR).reshape(GROUPS * SLOT, HEAD).astype(jnp.bfloat16)
        )
        u = lax.broadcasted_iota(jnp.int32, (KEYS, LANES), 0)
        t = lax.broadcasted_iota(jnp.int32, (KEYS, LANES), 1) % ROWS
        u_order = (u % ROWS) // SLOT * (CTX * SLOT) + u // ROWS * SLOT + u % SLOT
        t_order = t // SLOT * (CTX * SLOT) + me * SLOT + t % SLOT
        bias_ref[...] = jnp.where(u_order <= t_order, 0.0, -2.0 * FAR)
        vt_ref[HEAD:, :] = jnp.where(
            lax.broadcasted_iota(jnp.int32, (VALUE_ROWS - HEAD, BLOCKS * KEYS), 0) == 0, 1.0, 0.0
        ).astype(jnp.bfloat16)

    scale = math.log2(math.e) / math.sqrt(HEAD)
    queries = []
    for i in range(BLOCKS):
        at = slice(i * ROWS, (i + 1) * ROWS)
        mask = mask_ref[at, :]
        queries.append(
            jnp.concatenate(
                [
                    jnp.concatenate([q_ref[at, h * HEAD : (h + 1) * HEAD], mask], axis=1)
                    for h in range(PER_KV)
                ],
                axis=0,
            )
        )
    for b in range(BLOCKS):
        span = slice(b * SPAN, (b + 1) * SPAN)
        key = jnp.concatenate([k_ref[:, span].reshape(KEYS, HEAD), feat_ref[b]], axis=1)
        vt_ref[0:HEAD, b * KEYS : (b + 1) * KEYS] = jnp.transpose(
            v_ref[:, span].reshape(KEYS, HEAD).astype(jnp.float32)
        ).astype(jnp.bfloat16)
        for i in range(b, BLOCKS):
            s = lax.dot_general(
                key, queries[i], (((1,), (1,)), ((), ())), preferred_element_type=jnp.float32
            )
            s_ref[i, b] = s + bias_ref[...] if i == b else s
    for i in range(BLOCKS):
        top = jnp.max(s_ref[i, 0], axis=0, keepdims=True)
        for b in range(1, i + 1):
            top = jnp.maximum(top, jnp.max(s_ref[i, b], axis=0, keepdims=True))
        acc = None
        for b in range(i + 1):
            w = jnp.exp2((s_ref[i, b] - top) * scale).astype(jnp.bfloat16)
            part = jnp.dot(
                vt_ref[:, b * KEYS : (b + 1) * KEYS], w, preferred_element_type=jnp.float32
            )
            acc = part if acc is None else acc + part
        out = jnp.transpose(acc[0:HEAD] * (1.0 / acc[HEAD : HEAD + 1])).astype(jnp.bfloat16)
        for h in range(PER_KV):
            o_ref[i * ROWS : (i + 1) * ROWS, h * HEAD : (h + 1) * HEAD] = out[
                h * ROWS : (h + 1) * ROWS
            ]


def attend(lengths, me, q, kv, part):
    count = GROUPS * SLOT
    block = (CTX, GROUPS, SLOT, HEAD)
    low = part * HEADS
    return pl.pallas_call(
        attend_kernel,
        grid=(HEADS,),
        in_specs=[
            pl.BlockSpec(memory_space=pltpu.SMEM),
            pl.BlockSpec(memory_space=pltpu.SMEM),
            pl.BlockSpec((count, QW), lambda j: (0, j)),
            pl.BlockSpec(block, lambda j: (0, 0, 0, low + j)),
            pl.BlockSpec(block, lambda j: (0, 0, 0, KV_HEADS + low + j)),
        ],
        out_specs=pl.BlockSpec((count, QW), lambda j: (0, j)),
        out_shape=jax.ShapeDtypeStruct((count, HEADS * QW), jnp.bfloat16),
        scratch_shapes=[
            pltpu.VMEM((BLOCKS, KEYS, HEAD), jnp.bfloat16),
            pltpu.VMEM((count, HEAD), jnp.bfloat16),
            pltpu.VMEM((KEYS, LANES), jnp.float32),
            pltpu.VMEM((VALUE_ROWS, BLOCKS * KEYS), jnp.bfloat16),
            pltpu.VMEM((BLOCKS, BLOCKS, KEYS, LANES), jnp.float32),
        ],
        cost_estimate=pl.CostEstimate(
            flops=5 * 10**9, transcendentals=2 * 10**7, bytes_accessed=8 * 10**6
        ),
        name="attend",
    )(lengths, me, q, kv, kv)


def exchange(x):
    return lax.all_to_all(x, "dp", split_axis=0, concat_axis=0, tiled=True)


def gather(kv):
    return lax.all_gather(kv, "ctx", axis=0)


def body(query_rows, key_rows, token_values, group_of_row, doc_lengths):
    group = group_of_row.reshape(1, group_of_row.shape[0])
    me = lax.axis_index("ctx").astype(jnp.int32).reshape(1, 1)
    sent = pack_kv(group, key_rows, token_values)
    queries = pack_q(group, query_rows)
    kv, queries = lax.optimization_barrier((exchange(sent), queries))
    everyone = gather(kv)
    outs = []
    for part in range(PARTS):
        arrived = exchange(queries[part])
        if part + 1 < PARTS:
            arrived, queries = lax.optimization_barrier((arrived, queries))
        out = attend(doc_lengths, me, arrived.reshape(GROUPS * SLOT, HEADS * QW), everyone, part)
        outs.append(exchange(out.reshape(GROUPS, SLOT, HEADS * QW)))
    return unpack(group, outs)


def solution(mesh):
    rows = P(("dp", "ctx"), None)
    return jax.shard_map(
        body,
        mesh=mesh,
        in_specs=(rows, rows, rows, rows, P("dp", None)),
        out_specs=rows,
        check_vma=False,
    )
```

```python
import math

import jax
import jax.numpy as jnp
from jax import lax
from jax.experimental import pallas as pl
from jax.experimental.pallas import tpu as pltpu
from jax.sharding import PartitionSpec as P

KV_HEADS = 8
HEAD = 128
PER_KV = 4
GROUPS = 32
SLOT = 8
CTX = 8
QW = PER_KV * HEAD
EMPTY = 64.0
FAR = 16384.0
SPAN = 8
BLOCKS = GROUPS // SPAN
KEYS = CTX * SPAN * SLOT
ROWS = SPAN * SLOT
LANES = PER_KV * ROWS
VALUE_ROWS = HEAD + 16
PARTS = 1
HEADS = KV_HEADS // PARTS


def slot_targets(group_row):
    rows = group_row.shape[1]
    row = jnp.broadcast_to(group_row.astype(jnp.float32), (rows, rows))
    col = jnp.transpose(row)
    earlier = lax.broadcasted_iota(jnp.int32, (rows, rows), 0) < lax.broadcasted_iota(
        jnp.int32, (rows, rows), 1
    )
    same = jnp.where((col == row) & earlier, 1.0, 0.0)
    position = jnp.sum(same, axis=0, keepdims=True)
    return row[0:1, :] * float(SLOT) + position


def selection(group_row):
    slots, rows = GROUPS * SLOT, group_row.shape[1]
    slot = lax.broadcasted_iota(jnp.int32, (slots, rows), 0).astype(jnp.float32)
    return jnp.where(slot == slot_targets(group_row), 1.0, 0.0)


def laid(x):
    return x.reshape(GROUPS, SLOT, x.shape[1]).astype(jnp.bfloat16)


def pack_kv_kernel(group_ref, k_ref, v_ref, out_ref):
    pick = selection(group_ref[...])
    empty = (1.0 - jnp.sum(pick, axis=1, keepdims=True)) * EMPTY
    pick = pick.astype(jnp.bfloat16)
    width = k_ref.shape[1]
    out_ref[:, :, 0:width] = laid(jnp.dot(pick, k_ref[...], preferred_element_type=jnp.float32))
    out_ref[:, :, width:] = laid(
        jnp.dot(pick, v_ref[...], preferred_element_type=jnp.float32) + empty
    )


def pack_kv(group, k, v):
    return pl.pallas_call(
        pack_kv_kernel,
        out_shape=jax.ShapeDtypeStruct((GROUPS, SLOT, 2 * k.shape[1]), jnp.bfloat16),
        name="pack_kv",
    )(group, k, v)


def pack_q_kernel(group_ref, q_ref, *refs):
    outs, pick_ref = refs[:-1], refs[-1]
    step = pl.program_id(0)

    @pl.when(step == 0)
    def _():
        pick_ref[...] = selection(group_ref[...]).astype(jnp.bfloat16)

    for part, out_ref in enumerate(outs):

        @pl.when(step == part)
        def _(out_ref=out_ref):
            out_ref[...] = laid(
                jnp.dot(pick_ref[...], q_ref[...], preferred_element_type=jnp.float32)
            )


def pack_q(group, q):
    rows, width = q.shape
    part = width // PARTS
    shape = (GROUPS, SLOT, part)
    return pl.pallas_call(
        pack_q_kernel,
        grid=(PARTS,),
        in_specs=[
            pl.BlockSpec((1, rows), lambda i: (0, 0)),
            pl.BlockSpec((rows, part), lambda i: (0, i)),
        ],
        out_specs=[pl.BlockSpec(shape, lambda i: (0, 0, 0))] * PARTS,
        out_shape=[jax.ShapeDtypeStruct(shape, jnp.bfloat16)] * PARTS,
        scratch_shapes=[pltpu.VMEM((GROUPS * SLOT, rows), jnp.bfloat16)],
        name="pack_q",
    )(group, q)


def unpack_kernel(group_ref, *refs):
    parts, out_ref = refs[:-1], refs[-1]
    pick = jnp.transpose(selection(group_ref[...])).astype(jnp.bfloat16)
    for i, ref in enumerate(parts):
        width = ref.shape[2]
        out_ref[:, i * width : (i + 1) * width] = jnp.dot(
            pick, ref[...].reshape(GROUPS * SLOT, width), preferred_element_type=jnp.float32
        ).astype(jnp.bfloat16)


def unpack(group, parts):
    return pl.pallas_call(
        unpack_kernel,
        out_shape=jax.ShapeDtypeStruct(
            (group.shape[1], sum(p.shape[2] for p in parts)), jnp.bfloat16
        ),
        name="unpack",
    )(group, *parts)


def attend_kernel(len_ref, who_ref, q_ref, *refs):
    k_refs, v_refs = refs[:CTX], refs[CTX : 2 * CTX]
    o_ref, feat_ref, mask_ref, bias_ref, vt_ref, s_ref = refs[2 * CTX :]

    @pl.when(pl.program_id(0) == 0)
    def _():
        who = [who_ref[0, c] for c in range(CTX)]
        first_len = len_ref[0, 0].astype(jnp.float32)
        shape = (GROUPS, SLOT, HEAD)
        lane = lax.broadcasted_iota(jnp.int32, shape, 2).astype(jnp.float32)
        slot = lax.broadcasted_iota(jnp.int32, shape, 1).astype(jnp.float32)
        used = [
            jnp.broadcast_to(
                jnp.where(v_refs[c][...].astype(jnp.float32)[:, :, 0:1] < 0.5 * EMPTY, 1.0, 0.0), shape
            )
            for c in range(CTX)
        ]
        number = [jnp.sum(u, axis=1) for u in used]
        before = jnp.where(
            lax.broadcasted_iota(jnp.int32, (GROUPS, GROUPS), 0)
            > lax.broadcasted_iota(jnp.int32, (GROUPS, GROUPS), 1),
            1.0,
            0.0,
        )
        base = jnp.dot(
            before.astype(jnp.bfloat16),
            sum(number).astype(jnp.bfloat16),
            preferred_element_type=jnp.float32,
        )
        for c in range(CTX):
            earlier = sum(jnp.where(who[d] < who[c], number[d], 0.0) for d in range(CTX))
            rank = (base + earlier)[:, None, :] + slot
            code = jnp.where(used[c] > 0.5, jnp.where(rank < first_len, 0.0, 1.0), 2.0)
            if c == 0:
                mask_ref[...] = (
                    jnp.where(lane == code, 0.0, -FAR)
                    .reshape(GROUPS * SLOT, HEAD)
                    .astype(jnp.bfloat16)
                )
            feat = jnp.where(lane == code, 1.0, 0.0)
            for b in range(BLOCKS):
                feat_ref[b, c * ROWS : (c + 1) * ROWS, :] = (
                    feat[b * SPAN : (b + 1) * SPAN].reshape(ROWS, HEAD).astype(jnp.bfloat16)
                )
        u = lax.broadcasted_iota(jnp.int32, (ROWS, LANES), 0)
        t = lax.broadcasted_iota(jnp.int32, (ROWS, LANES), 1) % ROWS
        u_order = u // SLOT * (CTX * SLOT) + u % SLOT
        t_order = t // SLOT * (CTX * SLOT) + who[0] * SLOT + t % SLOT
        for c in range(CTX):
            bias_ref[c * ROWS : (c + 1) * ROWS, :] = jnp.where(
                u_order + who[c] * SLOT <= t_order, 0.0, -2.0 * FAR
            )
        vt_ref[HEAD:, :] = jnp.where(
            lax.broadcasted_iota(jnp.int32, (VALUE_ROWS - HEAD, BLOCKS * KEYS), 0) == 0, 1.0, 0.0
        ).astype(jnp.bfloat16)

    def joined(refs, span):
        return jnp.concatenate([ref[span].reshape(ROWS, HEAD) for ref in refs], axis=0)

    scale = math.log2(math.e) / math.sqrt(HEAD)
    queries = []
    for i in range(BLOCKS):
        at = slice(i * ROWS, (i + 1) * ROWS)
        mask = mask_ref[at, :]
        queries.append(
            jnp.concatenate(
                [
                    jnp.concatenate([q_ref[at, h * HEAD : (h + 1) * HEAD], mask], axis=1)
                    for h in range(PER_KV)
                ],
                axis=0,
            )
        )
    for b in range(BLOCKS):
        span = slice(b * SPAN, (b + 1) * SPAN)
        key = jnp.concatenate([joined(k_refs, span), feat_ref[b]], axis=1)
        vt_ref[0:HEAD, b * KEYS : (b + 1) * KEYS] = jnp.transpose(
            joined(v_refs, span).astype(jnp.float32)
        ).astype(jnp.bfloat16)
        for i in range(b, BLOCKS):
            s = lax.dot_general(
                key, queries[i], (((1,), (1,)), ((), ())), preferred_element_type=jnp.float32
            )
            s_ref[i, b] = s + bias_ref[...] if i == b else s
    for i in range(BLOCKS):
        top = jnp.max(s_ref[i, 0], axis=0, keepdims=True)
        for b in range(1, i + 1):
            top = jnp.maximum(top, jnp.max(s_ref[i, b], axis=0, keepdims=True))
        acc = None
        for b in range(i + 1):
            w = jnp.exp2((s_ref[i, b] - top) * scale).astype(jnp.bfloat16)
            part = jnp.dot(
                vt_ref[:, b * KEYS : (b + 1) * KEYS], w, preferred_element_type=jnp.float32
            )
            acc = part if acc is None else acc + part
        out = jnp.transpose(acc[0:HEAD] * (1.0 / acc[HEAD : HEAD + 1])).astype(jnp.bfloat16)
        for h in range(PER_KV):
            o_ref[i * ROWS : (i + 1) * ROWS, h * HEAD : (h + 1) * HEAD] = out[
                h * ROWS : (h + 1) * ROWS
            ]


def attend(lengths, who, q, keys, values):
    count = GROUPS * SLOT

    def heads(first):
        return pl.BlockSpec((GROUPS, SLOT, HEAD), lambda j: (0, 0, first + j))

    blocks = keys + values
    return pl.pallas_call(
        attend_kernel,
        grid=(HEADS,),
        in_specs=[
            pl.BlockSpec(memory_space=pltpu.SMEM),
            pl.BlockSpec(memory_space=pltpu.SMEM),
            pl.BlockSpec((count, QW), lambda j: (0, j)),
            *(heads(first) for _, first in blocks),
        ],
        out_specs=pl.BlockSpec((count, QW), lambda j: (0, j)),
        out_shape=jax.ShapeDtypeStruct((count, HEADS * QW), jnp.bfloat16),
        scratch_shapes=[
            pltpu.VMEM((BLOCKS, KEYS, HEAD), jnp.bfloat16),
            pltpu.VMEM((count, HEAD), jnp.bfloat16),
            pltpu.VMEM((KEYS, LANES), jnp.float32),
            pltpu.VMEM((VALUE_ROWS, BLOCKS * KEYS), jnp.bfloat16),
            pltpu.VMEM((BLOCKS, BLOCKS, KEYS, LANES), jnp.float32),
        ],
        cost_estimate=pl.CostEstimate(
            flops=10**10, transcendentals=4 * 10**7, bytes_accessed=16 * 10**6
        ),
        name="attend",
    )(lengths, who, q, *(array for array, _ in blocks))


def exchange(x):
    return lax.all_to_all(x, "dp", split_axis=0, concat_axis=0, tiled=True)


def gather(kv):
    me = lax.axis_index("ctx").astype(jnp.int32)
    right = [(i, (i + 2) % CTX) for i in range(CTX)]
    left = [(i, (i - 2) % CTX) for i in range(CTX)]
    across = [(i, i ^ 1) for i in range(CTX)]
    half = kv.shape[2] // 2
    before = lax.ppermute(kv, "ctx", right)
    after = lax.ppermute(kv, "ctx", left)
    far_keys = lax.ppermute(before[:, :, 0:half], "ctx", right)
    far_values = lax.ppermute(after[:, :, half:], "ctx", left)
    mine = (kv, before, after, far_keys, far_values)
    keys, values = [], []
    for side in (mine, tuple(lax.ppermute(x, "ctx", across) for x in mine)):
        keys += [(x, 0) for x in side[:4]]
        values += [(x, KV_HEADS) for x in side[:3]] + [(side[4], 0)]
    chip, core = me // 2, me % 2
    who = [(chip + d) % (CTX // 2) * 2 + core for d in (0, 3, 1, 2)]
    who = jnp.stack(who + [w + 1 - 2 * core for w in who]).reshape(1, CTX)
    return keys, values, who


def body(query_rows, key_rows, token_values, group_of_row, doc_lengths):
    group = group_of_row.reshape(1, group_of_row.shape[0])
    sent = pack_kv(group, key_rows, token_values)
    (queries,) = pack_q(group, query_rows)
    kv, queries = lax.optimization_barrier((exchange(sent), queries))
    keys, values, who = gather(kv)
    arrived = exchange(queries).reshape(GROUPS * SLOT, HEADS * QW)
    out = attend(doc_lengths, who, arrived, keys, values)
    return unpack(group, [exchange(out.reshape(GROUPS, SLOT, HEADS * QW))])


def solution(mesh):
    rows = P(("dp", "ctx"), None)
    return jax.shard_map(
        body,
        mesh=mesh,
        in_specs=(rows, rows, rows, rows, P("dp", None)),
        out_specs=rows,
        check_vma=False,
    )
```

```python
import math

import jax
import jax.numpy as jnp
from jax import lax
from jax.experimental import pallas as pl
from jax.experimental.pallas import tpu as pltpu
from jax.sharding import PartitionSpec as P

KV_HEADS = 8
HEAD = 128
PER_KV = 4
GROUPS = 32
SLOT = 8
QW = PER_KV * HEAD
ROW_W = QW + 2 * HEAD
EMPTY = 64.0
FAR = 16384.0
BLOCKS = 4
KEYS = 512
ROWS = 64
LANES = PER_KV * ROWS
GRANT = 24 << 20
VALUE_ROWS = HEAD + 16
STEP = 2


def slot_targets(group_row):
    rows = group_row.shape[1]
    row = jnp.broadcast_to(group_row.astype(jnp.float32), (rows, rows))
    col = jnp.transpose(row)
    earlier = lax.broadcasted_iota(jnp.int32, (rows, rows), 0) < lax.broadcasted_iota(
        jnp.int32, (rows, rows), 1
    )
    same = jnp.where((col == row) & earlier, 1.0, 0.0)
    position = jnp.sum(same, axis=0, keepdims=True)
    return row[0:1, :] * float(SLOT) + position


def pack_kernel(group_ref, q_ref, k_ref, v_ref, out_ref, pick_ref):
    slots = GROUPS * SLOT
    rows = q_ref.shape[0]

    @pl.when(pl.program_id(0) == 0)
    def _():
        target = slot_targets(group_ref[...])
        slot = lax.broadcasted_iota(jnp.int32, (slots, rows), 0).astype(jnp.float32)
        pick_ref[...] = jnp.where(slot == target, 1.0, 0.0).astype(jnp.bfloat16)

    pick = pick_ref[...]

    def moved(x):
        return jnp.dot(pick, x, preferred_element_type=jnp.float32)

    def laid(x):
        return x.reshape(GROUPS, SLOT, x.shape[1]).astype(jnp.bfloat16)

    empty = (1.0 - jnp.sum(pick.astype(jnp.float32), axis=1, keepdims=True)) * EMPTY
    for j in range(STEP):
        head = slice(j * HEAD, (j + 1) * HEAD)
        out_ref[:, j, :, 0:QW] = laid(moved(q_ref[:, j * QW : (j + 1) * QW]))
        out_ref[:, j, :, QW : QW + HEAD] = laid(moved(k_ref[:, head]))
        out_ref[:, j, :, QW + HEAD :] = laid(moved(v_ref[:, head]) + empty)


def pack(group, q, k, v):
    rows = q.shape[0]
    return pl.pallas_call(
        pack_kernel,
        grid=(KV_HEADS // STEP,),
        in_specs=[
            pl.BlockSpec((1, rows), lambda j: (0, 0)),
            pl.BlockSpec((rows, STEP * QW), lambda j: (0, j)),
            pl.BlockSpec((rows, STEP * HEAD), lambda j: (0, j)),
            pl.BlockSpec((rows, STEP * HEAD), lambda j: (0, j)),
        ],
        out_specs=pl.BlockSpec((GROUPS, STEP, SLOT, ROW_W), lambda j: (0, j, 0, 0)),
        out_shape=jax.ShapeDtypeStruct((GROUPS, KV_HEADS, SLOT, ROW_W), jnp.bfloat16),
        scratch_shapes=[pltpu.VMEM((GROUPS * SLOT, rows), jnp.bfloat16)],
        compiler_params=pltpu.CompilerParams(vmem_limit_bytes=GRANT),
        name="pack",
    )(group, q, k, v)


def unpack_kernel(group_ref, o_ref, out_ref, pick_ref):
    slots = GROUPS * SLOT
    rows = out_ref.shape[0]

    @pl.when(pl.program_id(0) == 0)
    def _():
        target = slot_targets(group_ref[...])
        slot = lax.broadcasted_iota(jnp.int32, (slots, rows), 0).astype(jnp.float32)
        pick_ref[...] = jnp.transpose(jnp.where(slot == target, 1.0, 0.0)).astype(jnp.bfloat16)

    for j in range(STEP):
        x = o_ref[:, j].reshape(slots, QW)
        out_ref[:, j * QW : (j + 1) * QW] = jnp.dot(
            pick_ref[...], x, preferred_element_type=jnp.float32
        ).astype(jnp.bfloat16)


def unpack(group, o):
    rows = group.shape[1]
    return pl.pallas_call(
        unpack_kernel,
        grid=(KV_HEADS // STEP,),
        in_specs=[
            pl.BlockSpec((1, rows), lambda j: (0, 0)),
            pl.BlockSpec((GROUPS, STEP, SLOT, QW), lambda j: (0, j, 0, 0)),
        ],
        out_specs=pl.BlockSpec((rows, STEP * QW), lambda j: (0, j)),
        out_shape=jax.ShapeDtypeStruct((rows, KV_HEADS * QW), jnp.bfloat16),
        scratch_shapes=[pltpu.VMEM((rows, GROUPS * SLOT), jnp.bfloat16)],
        compiler_params=pltpu.CompilerParams(vmem_limit_bytes=GRANT),
        name="unpack",
    )(group, o)


def attend_kernel(len_ref, q_ref, k_ref, v_ref, o_ref, feat_ref, mask_ref, ahead_ref, vt_ref, s_ref):
    count = k_ref.shape[0]
    step = pl.program_id(0)

    @pl.when(step == 0)
    def _():
        first_len = len_ref[0, 0].astype(jnp.float32)
        sources = count // SLOT
        shape = (sources, SLOT, HEAD)
        lane = lax.broadcasted_iota(jnp.int32, shape, 2).astype(jnp.float32)
        slot = lax.broadcasted_iota(jnp.int32, shape, 1).astype(jnp.float32)
        value = v_ref[...].astype(jnp.float32)
        used = jnp.broadcast_to(
            jnp.where(value.reshape(shape)[:, :, 0:1] < 0.5 * EMPTY, 1.0, 0.0), shape
        )
        before = jnp.where(
            lax.broadcasted_iota(jnp.int32, (sources, sources), 0)
            > lax.broadcasted_iota(jnp.int32, (sources, sources), 1),
            1.0,
            0.0,
        )
        base = jnp.dot(
            before.astype(jnp.bfloat16),
            jnp.sum(used, axis=1).astype(jnp.bfloat16),
            preferred_element_type=jnp.float32,
        )
        rank = base[:, None, :] + slot
        code = jnp.where(used > 0.5, jnp.where(rank < first_len, 0.0, 1.0), 2.0)
        hit = lane == code
        feat_ref[...] = jnp.where(hit, 1.0, 0.0).reshape(count, HEAD).astype(jnp.bfloat16)
        mask_ref[...] = jnp.where(hit, 0.0, -FAR).reshape(mask_ref.shape).astype(jnp.bfloat16)
        ahead_ref[...] = (
            lax.broadcasted_iota(jnp.int32, (KEYS, LANES), 0)
            - lax.broadcasted_iota(jnp.int32, (KEYS, LANES), 1) % ROWS
        ).astype(jnp.float32)
        vt_ref[0:HEAD, :] = jnp.transpose(value).astype(jnp.bfloat16)
        vt_ref[HEAD:, :] = jnp.where(
            lax.broadcasted_iota(jnp.int32, (VALUE_ROWS - HEAD, count), 0) == 0, 1.0, 0.0
        ).astype(jnp.bfloat16)

    scale = math.log2(math.e) / math.sqrt(HEAD)
    offset = pl.multiple_of(step * ROWS, ROWS)
    bias = jnp.where(ahead_ref[...] <= offset.astype(jnp.float32), 0.0, -2.0 * FAR)
    queries = []
    for i in range(BLOCKS):
        mask = mask_ref[i, pl.ds(offset, ROWS), :]
        queries.append(
            jnp.concatenate(
                [
                    jnp.concatenate([q_ref[i, :, h * HEAD : (h + 1) * HEAD], mask], axis=1)
                    for h in range(PER_KV)
                ],
                axis=0,
            )
        )
    for b in range(BLOCKS):
        at = slice(b * KEYS, (b + 1) * KEYS)
        key = jnp.concatenate([k_ref[at, :], feat_ref[at, :]], axis=1)
        for i in range(b, BLOCKS):
            s = lax.dot_general(
                key, queries[i], (((1,), (1,)), ((), ())), preferred_element_type=jnp.float32
            )
            s_ref[i * (i + 1) // 2 + b] = s + bias if i == b else s
    for i in range(BLOCKS):
        low = i * (i + 1) // 2
        top = jnp.max(s_ref[low], axis=0, keepdims=True)
        for b in range(1, i + 1):
            top = jnp.maximum(top, jnp.max(s_ref[low + b], axis=0, keepdims=True))
        acc = None
        for b in range(i + 1):
            w = jnp.exp2((s_ref[low + b] - top) * scale).astype(jnp.bfloat16)
            part = jnp.dot(
                vt_ref[:, b * KEYS : (b + 1) * KEYS], w, preferred_element_type=jnp.float32
            )
            acc = part if acc is None else acc + part
        out = jnp.transpose(acc[0:HEAD] * (1.0 / acc[HEAD : HEAD + 1])).astype(jnp.bfloat16)
        for h in range(PER_KV):
            o_ref[i, :, h * HEAD : (h + 1) * HEAD] = out[h * ROWS : (h + 1) * ROWS]


def attend(lengths, rows):
    count = rows.shape[0]
    tile = pl.BlockSpec((BLOCKS, ROWS, QW), lambda i: (0, i, 0))
    out = pl.pallas_call(
        attend_kernel,
        grid=(KEYS // ROWS,),
        in_specs=[
            pl.BlockSpec(memory_space=pltpu.SMEM),
            tile,
            pl.BlockSpec((count, HEAD), lambda i: (0, PER_KV)),
            pl.BlockSpec((count, HEAD), lambda i: (0, PER_KV + 1)),
        ],
        out_specs=tile,
        out_shape=jax.ShapeDtypeStruct((BLOCKS, KEYS, QW), jnp.bfloat16),
        scratch_shapes=[
            pltpu.VMEM((count, HEAD), jnp.bfloat16),
            pltpu.VMEM((BLOCKS, KEYS, HEAD), jnp.bfloat16),
            pltpu.VMEM((KEYS, LANES), jnp.float32),
            pltpu.VMEM((VALUE_ROWS, count), jnp.bfloat16),
            pltpu.VMEM((BLOCKS * (BLOCKS + 1) // 2, KEYS, LANES), jnp.float32),
        ],
        compiler_params=pltpu.CompilerParams(vmem_limit_bytes=GRANT),
        name="attend",
    )(lengths, rows.reshape(BLOCKS, KEYS, ROW_W), rows, rows)
    return out.reshape(count, QW)


def body(query_rows, key_rows, token_values, group_of_row, doc_lengths):
    devices = lax.axis_size("dp") * lax.axis_size("ctx")
    group = group_of_row.reshape(1, group_of_row.shape[0])
    packed = pack(group, query_rows, key_rows, token_values)
    arrived = lax.all_to_all(
        packed.reshape(devices, SLOT, ROW_W), ("dp", "ctx"), split_axis=0, concat_axis=0, tiled=True
    )
    result = attend(doc_lengths, arrived.reshape(devices * SLOT, ROW_W))
    returned = lax.all_to_all(
        result.reshape(devices, SLOT, QW), ("dp", "ctx"), split_axis=0, concat_axis=0, tiled=True
    )
    return unpack(group, returned.reshape(GROUPS, KV_HEADS, SLOT, QW))


def solution(mesh):
    rows = P(("dp", "ctx"), None)
    return jax.shard_map(
        body,
        mesh=mesh,
        in_specs=(rows, rows, rows, rows, P("dp", None)),
        out_specs=rows,
        check_vma=False,
    )
```

```python
import math

import jax
import jax.numpy as jnp
from jax import lax
from jax.experimental import pallas as pl
from jax.experimental.pallas import tpu as pltpu
from jax.sharding import PartitionSpec as P

KV_HEADS = 8
HEAD = 128
PER_KV = 4
GROUPS = 32
SLOT = 8
QW = PER_KV * HEAD
ROW_W = QW + 2 * HEAD
EMPTY = 64.0
FAR = 16384.0
BLOCKS = 4
KEYS = 512
ROWS = 64
LANES = PER_KV * ROWS
CTX = 8
PART = BLOCKS * ROWS
GRANT = 24 << 20
VALUE_ROWS = HEAD + 16
STEP = 2


def slot_targets(group_row):
    rows = group_row.shape[1]
    row = jnp.broadcast_to(group_row.astype(jnp.float32), (rows, rows))
    col = jnp.transpose(row)
    earlier = lax.broadcasted_iota(jnp.int32, (rows, rows), 0) < lax.broadcasted_iota(
        jnp.int32, (rows, rows), 1
    )
    same = jnp.where((col == row) & earlier, 1.0, 0.0)
    position = jnp.sum(same, axis=0, keepdims=True)
    return row[0:1, :] * float(SLOT) + position


def pack_kernel(group_ref, q_ref, k_ref, v_ref, out_ref, pick_ref):
    slots = GROUPS * SLOT
    rows = q_ref.shape[0]

    @pl.when(pl.program_id(0) == 0)
    def _():
        target = slot_targets(group_ref[...])
        slot = lax.broadcasted_iota(jnp.int32, (slots, rows), 0).astype(jnp.float32)
        pick_ref[...] = jnp.where(slot == target, 1.0, 0.0).astype(jnp.bfloat16)

    pick = pick_ref[...]

    def moved(x):
        return jnp.dot(pick, x, preferred_element_type=jnp.float32)

    def laid(x):
        return x.reshape(GROUPS, SLOT, x.shape[1]).astype(jnp.bfloat16)

    empty = (1.0 - jnp.sum(pick.astype(jnp.float32), axis=1, keepdims=True)) * EMPTY
    for j in range(STEP):
        head = slice(j * HEAD, (j + 1) * HEAD)
        out_ref[j, :, :, 0:QW] = laid(moved(q_ref[:, j * QW : (j + 1) * QW]))
        out_ref[j, :, :, QW : QW + HEAD] = laid(moved(k_ref[:, head]))
        out_ref[j, :, :, QW + HEAD :] = laid(moved(v_ref[:, head]) + empty)


def pack(group, q, k, v):
    rows = q.shape[0]
    return pl.pallas_call(
        pack_kernel,
        grid=(KV_HEADS // STEP,),
        in_specs=[
            pl.BlockSpec((1, rows), lambda j: (0, 0)),
            pl.BlockSpec((rows, STEP * QW), lambda j: (0, j)),
            pl.BlockSpec((rows, STEP * HEAD), lambda j: (0, j)),
            pl.BlockSpec((rows, STEP * HEAD), lambda j: (0, j)),
        ],
        out_specs=pl.BlockSpec((STEP, GROUPS, SLOT, ROW_W), lambda j: (j, 0, 0, 0)),
        out_shape=jax.ShapeDtypeStruct((KV_HEADS, GROUPS, SLOT, ROW_W), jnp.bfloat16),
        scratch_shapes=[pltpu.VMEM((GROUPS * SLOT, rows), jnp.bfloat16)],
        compiler_params=pltpu.CompilerParams(vmem_limit_bytes=GRANT),
        name="pack",
    )(group, *(pltpu.with_memory_space_constraint(x, pltpu.HBM) for x in (q, k, v)))


def unpack_kernel(group_ref, o_ref, out_ref, pick_ref):
    slots = GROUPS * SLOT
    rows = out_ref.shape[0]

    @pl.when(pl.program_id(0) == 0)
    def _():
        target = slot_targets(group_ref[...])
        slot = lax.broadcasted_iota(jnp.int32, (slots, rows), 0).astype(jnp.float32)
        pick_ref[...] = jnp.transpose(jnp.where(slot == target, 1.0, 0.0)).astype(jnp.bfloat16)

    for j in range(STEP):
        x = o_ref[j].reshape(slots, QW)
        out_ref[:, j * QW : (j + 1) * QW] = jnp.dot(
            pick_ref[...], x, preferred_element_type=jnp.float32
        ).astype(jnp.bfloat16)


def unpack(group, o):
    rows = group.shape[1]
    return pl.pallas_call(
        unpack_kernel,
        grid=(KV_HEADS // STEP,),
        in_specs=[
            pl.BlockSpec((1, rows), lambda j: (0, 0)),
            pl.BlockSpec((STEP, GROUPS, SLOT, QW), lambda j: (j, 0, 0, 0)),
        ],
        out_specs=pl.BlockSpec((rows, STEP * QW), lambda j: (0, j)),
        out_shape=jax.ShapeDtypeStruct((rows, KV_HEADS * QW), jnp.bfloat16),
        scratch_shapes=[pltpu.VMEM((rows, GROUPS * SLOT), jnp.bfloat16)],
        compiler_params=pltpu.CompilerParams(vmem_limit_bytes=GRANT),
        name="unpack",
    )(group, o)


def attend_kernel(len_ref, q_ref, k_ref, v_ref, o_ref, feat_ref, mask_ref, ahead_ref, vt_ref, s_ref):
    count = k_ref.shape[0]
    step = pl.program_id(0)

    def joined(ref, b):
        low = b * ROWS
        return jnp.concatenate(
            [ref[c * PART + low : c * PART + low + ROWS, :] for c in range(CTX)], axis=0
        )

    @pl.when(step == 0)
    def _():
        first_len = len_ref[0, 0].astype(jnp.float32)
        shape = (GROUPS, SLOT, HEAD)
        lane = lax.broadcasted_iota(jnp.int32, shape, 2).astype(jnp.float32)
        slot = lax.broadcasted_iota(jnp.int32, shape, 1).astype(jnp.float32)
        value = v_ref[...].astype(jnp.float32)
        used = [
            jnp.broadcast_to(
                jnp.where(part.reshape(shape)[:, :, 0:1] < 0.5 * EMPTY, 1.0, 0.0), shape
            )
            for part in (value[c * PART : (c + 1) * PART] for c in range(CTX))
        ]
        number = [jnp.sum(u, axis=1) for u in used]
        before = jnp.where(
            lax.broadcasted_iota(jnp.int32, (GROUPS, GROUPS), 0)
            > lax.broadcasted_iota(jnp.int32, (GROUPS, GROUPS), 1),
            1.0,
            0.0,
        )
        base = jnp.dot(
            before.astype(jnp.bfloat16),
            sum(number).astype(jnp.bfloat16),
            preferred_element_type=jnp.float32,
        )
        for c in range(CTX):
            rank = base[:, None, :] + slot
            base = base + number[c]
            code = jnp.where(used[c] > 0.5, jnp.where(rank < first_len, 0.0, 1.0), 2.0)
            hit = lane == code
            at = slice(c * PART, (c + 1) * PART)
            feat_ref[at, :] = jnp.where(hit, 1.0, 0.0).reshape(PART, HEAD).astype(jnp.bfloat16)
            mask_ref[at, :] = jnp.where(hit, 0.0, -FAR).reshape(PART, HEAD).astype(jnp.bfloat16)
        u = lax.broadcasted_iota(jnp.int32, (KEYS, LANES), 0)
        t = lax.broadcasted_iota(jnp.int32, (KEYS, LANES), 1) % ROWS
        u_order = u % ROWS // SLOT * (CTX * SLOT) + u // ROWS * SLOT + u % SLOT
        ahead_ref[...] = (u_order - t // SLOT * (CTX * SLOT) - t % SLOT).astype(jnp.float32)
        for b in range(BLOCKS):
            vt_ref[0:HEAD, b * KEYS : (b + 1) * KEYS] = jnp.transpose(joined(value, b)).astype(
                jnp.bfloat16
            )
        vt_ref[HEAD:, :] = jnp.where(
            lax.broadcasted_iota(jnp.int32, (VALUE_ROWS - HEAD, count), 0) == 0, 1.0, 0.0
        ).astype(jnp.bfloat16)

    scale = math.log2(math.e) / math.sqrt(HEAD)
    bias = jnp.where(ahead_ref[...] <= (step * SLOT).astype(jnp.float32), 0.0, -2.0 * FAR)

    queries = []
    for i in range(BLOCKS):
        mask = mask_ref[pl.ds(pl.multiple_of(step * PART + i * ROWS, ROWS), ROWS), :]
        queries.append(
            jnp.concatenate(
                [
                    jnp.concatenate([q_ref[0, i, :, h * HEAD : (h + 1) * HEAD], mask], axis=1)
                    for h in range(PER_KV)
                ],
                axis=0,
            )
        )
    for b in range(BLOCKS):
        key = jnp.concatenate([joined(k_ref, b), joined(feat_ref, b)], axis=1)
        for i in range(b, BLOCKS):
            s = lax.dot_general(
                key, queries[i], (((1,), (1,)), ((), ())), preferred_element_type=jnp.float32
            )
            s_ref[i * (i + 1) // 2 + b] = s + bias if i == b else s
    for i in range(BLOCKS):
        low = i * (i + 1) // 2
        top = jnp.max(s_ref[low], axis=0, keepdims=True)
        for b in range(1, i + 1):
            top = jnp.maximum(top, jnp.max(s_ref[low + b], axis=0, keepdims=True))
        acc = None
        for b in range(i + 1):
            w = jnp.exp2((s_ref[low + b] - top) * scale).astype(jnp.bfloat16)
            part = jnp.dot(
                vt_ref[:, b * KEYS : (b + 1) * KEYS], w, preferred_element_type=jnp.float32
            )
            acc = part if acc is None else acc + part
        out = jnp.transpose(acc[0:HEAD] * (1.0 / acc[HEAD : HEAD + 1])).astype(jnp.bfloat16)
        for h in range(PER_KV):
            o_ref[0, i, :, h * HEAD : (h + 1) * HEAD] = out[h * ROWS : (h + 1) * ROWS]


def attend(lengths, rows):
    count = rows.shape[0]
    tile = pl.BlockSpec((1, BLOCKS, ROWS, QW), lambda c: (c, 0, 0, 0))
    out = pl.pallas_call(
        attend_kernel,
        grid=(CTX,),
        in_specs=[
            pl.BlockSpec(memory_space=pltpu.SMEM),
            tile,
            pl.BlockSpec((count, HEAD), lambda i: (0, PER_KV)),
            pl.BlockSpec((count, HEAD), lambda i: (0, PER_KV + 1)),
        ],
        out_specs=tile,
        out_shape=jax.ShapeDtypeStruct((CTX, BLOCKS, ROWS, QW), jnp.bfloat16),
        scratch_shapes=[
            pltpu.VMEM((count, HEAD), jnp.bfloat16),
            pltpu.VMEM((count, HEAD), jnp.bfloat16),
            pltpu.VMEM((KEYS, LANES), jnp.float32),
            pltpu.VMEM((VALUE_ROWS, count), jnp.bfloat16),
            pltpu.VMEM((BLOCKS * (BLOCKS + 1) // 2, KEYS, LANES), jnp.float32),
        ],
        compiler_params=pltpu.CompilerParams(vmem_limit_bytes=GRANT),
        name="attend",
    )(lengths, rows.reshape(CTX, BLOCKS, ROWS, ROW_W), rows, rows)
    return out.reshape(count, QW)


def body(query_rows, key_rows, token_values, group_of_row, doc_lengths):
    devices = lax.axis_size("dp") * lax.axis_size("ctx")
    group = group_of_row.reshape(1, group_of_row.shape[0])
    packed = pack(group, query_rows, key_rows, token_values)
    arrived = lax.all_to_all(
        packed.reshape(devices, SLOT, ROW_W), ("ctx", "dp"), split_axis=0, concat_axis=0, tiled=True
    )
    result = attend(doc_lengths, arrived.reshape(devices * SLOT, ROW_W))
    returned = lax.all_to_all(
        result.reshape(devices, SLOT, QW), ("ctx", "dp"), split_axis=0, concat_axis=0, tiled=True
    )
    return unpack(group, returned.reshape(KV_HEADS, GROUPS, SLOT, QW))


def solution(mesh):
    rows = P(("dp", "ctx"), None)
    return jax.shard_map(
        body,
        mesh=mesh,
        in_specs=(rows, rows, rows, rows, P("dp", None)),
        out_specs=rows,
        check_vma=False,
    )
```

```python
import math

import jax
import jax.numpy as jnp
from jax import lax
from jax.experimental import pallas as pl
from jax.experimental.pallas import tpu as pltpu
from jax.sharding import PartitionSpec as P

KV_HEADS = 8
HEAD = 128
PER_KV = 4
GROUPS = 32
SLOT = 8
CTX = 8
QW = PER_KV * HEAD
EMPTY = 64.0
FAR = 16384.0
SPAN = 8
BLOCKS = GROUPS // SPAN
KEYS = CTX * SPAN * SLOT
ROWS = SPAN * SLOT
LANES = PER_KV * ROWS
VALUE_ROWS = HEAD + 16
PARTS = (2, 6)
GRANT = 28 << 20


def slot_targets(group_row):
    rows = group_row.shape[1]
    row = jnp.broadcast_to(group_row.astype(jnp.float32), (rows, rows))
    col = jnp.transpose(row)
    earlier = lax.broadcasted_iota(jnp.int32, (rows, rows), 0) < lax.broadcasted_iota(
        jnp.int32, (rows, rows), 1
    )
    same = jnp.where((col == row) & earlier, 1.0, 0.0)
    position = jnp.sum(same, axis=0, keepdims=True)
    return row[0:1, :] * float(SLOT) + position


def selection(group_row):
    slots, rows = GROUPS * SLOT, group_row.shape[1]
    slot = lax.broadcasted_iota(jnp.int32, (slots, rows), 0).astype(jnp.float32)
    return jnp.where(slot == slot_targets(group_row), 1.0, 0.0)


def laid(x):
    return x.reshape(GROUPS, SLOT, x.shape[1]).astype(jnp.bfloat16)


def off_chip(x):
    return pltpu.with_memory_space_constraint(x, pltpu.HBM)


def pack_kv_kernel(group_ref, k_ref, v_ref, out_ref):
    pick = selection(group_ref[...])
    empty = (1.0 - jnp.sum(pick, axis=1, keepdims=True)) * EMPTY
    pick = pick.astype(jnp.bfloat16)
    width = k_ref.shape[1]
    out_ref[:, :, 0:width] = laid(jnp.dot(pick, k_ref[...], preferred_element_type=jnp.float32))
    out_ref[:, :, width:] = laid(
        jnp.dot(pick, v_ref[...], preferred_element_type=jnp.float32) + empty
    )


def pack_kv(group, k, v):
    return pl.pallas_call(
        pack_kv_kernel,
        out_shape=jax.ShapeDtypeStruct((GROUPS, SLOT, 2 * k.shape[1]), jnp.bfloat16),
        compiler_params=pltpu.CompilerParams(vmem_limit_bytes=GRANT),
        name="pack_kv",
    )(group, off_chip(k), off_chip(v))


def pack_q_kernel(group_ref, q_ref, out_ref, pick_ref):
    @pl.when(pl.program_id(0) == 0)
    def _():
        pick_ref[...] = selection(group_ref[...]).astype(jnp.bfloat16)

    out_ref[...] = laid(jnp.dot(pick_ref[...], q_ref[...], preferred_element_type=jnp.float32))


def pack_q(group, q):
    rows, width = q.shape
    part = 2 * QW
    return pl.pallas_call(
        pack_q_kernel,
        grid=(width // part,),
        in_specs=[
            pl.BlockSpec((1, rows), lambda i: (0, 0)),
            pl.BlockSpec((rows, part), lambda i: (0, i)),
        ],
        out_specs=pl.BlockSpec((GROUPS, SLOT, part), lambda i: (0, 0, i)),
        out_shape=jax.ShapeDtypeStruct((GROUPS, SLOT, width), jnp.bfloat16),
        scratch_shapes=[pltpu.VMEM((GROUPS * SLOT, rows), jnp.bfloat16)],
        compiler_params=pltpu.CompilerParams(vmem_limit_bytes=GRANT),
        name="pack_q",
    )(group, off_chip(q))


def unpack_kernel(group_ref, *refs):
    parts, out_ref = refs[:-1], refs[-1]
    pick = jnp.transpose(selection(group_ref[...])).astype(jnp.bfloat16)
    low = 0
    for ref in parts:
        width = ref.shape[2]
        out_ref[:, low : low + width] = jnp.dot(
            pick, ref[...].reshape(GROUPS * SLOT, width), preferred_element_type=jnp.float32
        ).astype(jnp.bfloat16)
        low += width


def unpack(group, parts):
    return pl.pallas_call(
        unpack_kernel,
        out_shape=jax.ShapeDtypeStruct(
            (group.shape[1], sum(p.shape[2] for p in parts)), jnp.bfloat16
        ),
        compiler_params=pltpu.CompilerParams(vmem_limit_bytes=GRANT),
        name="unpack",
    )(group, *parts)


def attend_kernel(len_ref, who_ref, q_ref, *refs):
    k_refs, v_refs = refs[:CTX], refs[CTX : 2 * CTX]
    o_ref, feat_ref, mask_ref, bias_ref, vt_ref, s_ref = refs[2 * CTX :]

    @pl.when(pl.program_id(0) == 0)
    def _():
        who = [who_ref[0, c] for c in range(CTX)]
        first_len = len_ref[0, 0].astype(jnp.float32)
        shape = (GROUPS, SLOT, HEAD)
        lane = lax.broadcasted_iota(jnp.int32, shape, 2).astype(jnp.float32)
        slot = lax.broadcasted_iota(jnp.int32, shape, 1).astype(jnp.float32)
        used = [
            jnp.broadcast_to(
                jnp.where(v_refs[c][...].astype(jnp.float32)[:, :, 0:1] < 0.5 * EMPTY, 1.0, 0.0), shape
            )
            for c in range(CTX)
        ]
        number = [jnp.sum(u, axis=1) for u in used]
        before = jnp.where(
            lax.broadcasted_iota(jnp.int32, (GROUPS, GROUPS), 0)
            > lax.broadcasted_iota(jnp.int32, (GROUPS, GROUPS), 1),
            1.0,
            0.0,
        )
        base = jnp.dot(
            before.astype(jnp.bfloat16),
            sum(number).astype(jnp.bfloat16),
            preferred_element_type=jnp.float32,
        )
        for c in range(CTX):
            earlier = sum(jnp.where(who[d] < who[c], number[d], 0.0) for d in range(CTX))
            rank = (base + earlier)[:, None, :] + slot
            code = jnp.where(used[c] > 0.5, jnp.where(rank < first_len, 0.0, 1.0), 2.0)
            if c == 0:
                mask_ref[...] = (
                    jnp.where(lane == code, 0.0, -FAR)
                    .reshape(GROUPS * SLOT, HEAD)
                    .astype(jnp.bfloat16)
                )
            feat = jnp.where(lane == code, 1.0, 0.0)
            for b in range(BLOCKS):
                feat_ref[b, c * ROWS : (c + 1) * ROWS, :] = (
                    feat[b * SPAN : (b + 1) * SPAN].reshape(ROWS, HEAD).astype(jnp.bfloat16)
                )
        u = lax.broadcasted_iota(jnp.int32, (ROWS, LANES), 0)
        t = lax.broadcasted_iota(jnp.int32, (ROWS, LANES), 1) % ROWS
        u_order = u // SLOT * (CTX * SLOT) + u % SLOT
        t_order = t // SLOT * (CTX * SLOT) + who[0] * SLOT + t % SLOT
        for c in range(CTX):
            bias_ref[c * ROWS : (c + 1) * ROWS, :] = jnp.where(
                u_order + who[c] * SLOT <= t_order, 0.0, -2.0 * FAR
            )
        vt_ref[HEAD:, :] = jnp.where(
            lax.broadcasted_iota(jnp.int32, (VALUE_ROWS - HEAD, BLOCKS * KEYS), 0) == 0, 1.0, 0.0
        ).astype(jnp.bfloat16)

    def place(i, b):
        return i * (i + 1) // 2 + b

    def joined(refs, span):
        return jnp.concatenate([ref[span].reshape(ROWS, HEAD) for ref in refs], axis=0)

    scale = math.log2(math.e) / math.sqrt(HEAD)
    queries = []
    for i in range(BLOCKS):
        at = slice(i * ROWS, (i + 1) * ROWS)
        mask = mask_ref[at, :]
        queries.append(
            jnp.concatenate(
                [
                    jnp.concatenate([q_ref[at, h * HEAD : (h + 1) * HEAD], mask], axis=1)
                    for h in range(PER_KV)
                ],
                axis=0,
            )
        )
    for b in range(BLOCKS):
        span = slice(b * SPAN, (b + 1) * SPAN)
        key = jnp.concatenate([joined(k_refs, span), feat_ref[b]], axis=1)
        vt_ref[0:HEAD, b * KEYS : (b + 1) * KEYS] = jnp.transpose(
            joined(v_refs, span).astype(jnp.float32)
        ).astype(jnp.bfloat16)
        for i in range(b, BLOCKS):
            s = lax.dot_general(
                key, queries[i], (((1,), (1,)), ((), ())), preferred_element_type=jnp.float32
            )
            s_ref[place(i, b)] = s + bias_ref[...] if i == b else s
    for i in range(BLOCKS):
        top = jnp.max(s_ref[place(i, 0)], axis=0, keepdims=True)
        for b in range(1, i + 1):
            top = jnp.maximum(top, jnp.max(s_ref[place(i, b)], axis=0, keepdims=True))
        acc = None
        for b in range(i + 1):
            w = jnp.exp2((s_ref[place(i, b)] - top) * scale).astype(jnp.bfloat16)
            part = jnp.dot(
                vt_ref[:, b * KEYS : (b + 1) * KEYS], w, preferred_element_type=jnp.float32
            )
            acc = part if acc is None else acc + part
        out = jnp.transpose(acc[0:HEAD] * (1.0 / acc[HEAD : HEAD + 1])).astype(jnp.bfloat16)
        for h in range(PER_KV):
            o_ref[i * ROWS : (i + 1) * ROWS, h * HEAD : (h + 1) * HEAD] = out[
                h * ROWS : (h + 1) * ROWS
            ]


def attend(lengths, who, q, keys, values, low, heads):
    count = GROUPS * SLOT

    def slabs(first):
        return pl.BlockSpec((GROUPS, SLOT, HEAD), lambda j: (0, 0, first + low + j))

    blocks = keys + values
    return pl.pallas_call(
        attend_kernel,
        grid=(heads,),
        in_specs=[
            pl.BlockSpec(memory_space=pltpu.SMEM),
            pl.BlockSpec(memory_space=pltpu.SMEM),
            pl.BlockSpec((count, QW), lambda j: (0, low + j)),
            *(slabs(first) for _, first in blocks),
        ],
        out_specs=pl.BlockSpec((count, QW), lambda j: (0, j)),
        out_shape=jax.ShapeDtypeStruct((count, heads * QW), jnp.bfloat16),
        scratch_shapes=[
            pltpu.VMEM((BLOCKS, KEYS, HEAD), jnp.bfloat16),
            pltpu.VMEM((count, HEAD), jnp.bfloat16),
            pltpu.VMEM((KEYS, LANES), jnp.float32),
            pltpu.VMEM((VALUE_ROWS, BLOCKS * KEYS), jnp.bfloat16),
            pltpu.VMEM((BLOCKS * (BLOCKS + 1) // 2, KEYS, LANES), jnp.float32),
        ],
        cost_estimate=pl.CostEstimate(
            flops=heads * 10**9, transcendentals=heads * 5 * 10**6, bytes_accessed=heads * 2 * 10**6
        ),
        name="attend",
    )(lengths, who, q, *(array for array, _ in blocks))


def exchange(x):
    return lax.all_to_all(x, "dp", split_axis=0, concat_axis=0, tiled=True)


def gather(kv):
    me = lax.axis_index("ctx").astype(jnp.int32)
    right = [(i, (i + 2) % CTX) for i in range(CTX)]
    left = [(i, (i - 2) % CTX) for i in range(CTX)]
    across = [(i, i ^ 1) for i in range(CTX)]
    half = kv.shape[2] // 2
    before = lax.ppermute(kv, "ctx", right)
    after = lax.ppermute(kv, "ctx", left)
    far_keys = lax.ppermute(before[:, :, 0:half], "ctx", right)
    far_values = lax.ppermute(after[:, :, half:], "ctx", left)
    mine = (kv, before, after, far_keys, far_values)
    keys, values = [], []
    for side in (mine, tuple(lax.ppermute(x, "ctx", across) for x in mine)):
        keys += [(x, 0) for x in side[:4]]
        values += [(x, KV_HEADS) for x in side[:3]] + [(side[4], 0)]
    chip, core = me // 2, me % 2
    who = [(chip + d) % (CTX // 2) * 2 + core for d in (0, 3, 1, 2)]
    who = jnp.stack(who + [w + 1 - 2 * core for w in who]).reshape(1, CTX)
    return keys, values, who


def body(query_rows, key_rows, token_values, group_of_row, doc_lengths):
    group = group_of_row.reshape(1, group_of_row.shape[0])
    sent = pack_kv(group, key_rows, token_values)
    queries = pack_q(group, query_rows)
    kv, queries = lax.optimization_barrier((exchange(sent), queries))
    keys, values, who = gather(kv)
    arrived = exchange(queries).reshape(GROUPS * SLOT, queries.shape[2])
    outs, low = [], 0
    for heads in PARTS:
        out = attend(doc_lengths, who, arrived, keys, values, low, heads)
        outs.append(exchange(out.reshape(GROUPS, SLOT, out.shape[1])))
        low += heads
    return unpack(group, outs)


def solution(mesh):
    rows = P(("dp", "ctx"), None)
    return jax.shard_map(
        body,
        mesh=mesh,
        in_specs=(rows, rows, rows, rows, P("dp", None)),
        out_specs=rows,
        check_vma=False,
    )
```

```python
import math

import jax
import jax.numpy as jnp
from jax import lax
from jax.experimental import pallas as pl
from jax.experimental.pallas import tpu as pltpu
from jax.sharding import PartitionSpec as P

KV_HEADS = 8
HEAD = 128
PER_KV = 4
GROUPS = 32
SLOT = 8
QW = PER_KV * HEAD
ROW_W = QW + 2 * HEAD
EMPTY = 64.0
FAR = 16384.0
BLOCKS = 4
KEYS = 512
ROWS = 64
LANES = PER_KV * ROWS
CTX = 8
PART = BLOCKS * ROWS
NEAR = ROWS // 2
HALF = KEYS // 2
SIDE = LANES // 2
GRANT = 24 << 20
VALUE_ROWS = HEAD + 16
STEP = 2


def slot_targets(group_row):
    rows = group_row.shape[1]
    row = jnp.broadcast_to(group_row.astype(jnp.float32), (rows, rows))
    col = jnp.transpose(row)
    earlier = lax.broadcasted_iota(jnp.int32, (rows, rows), 0) < lax.broadcasted_iota(
        jnp.int32, (rows, rows), 1
    )
    same = jnp.where((col == row) & earlier, 1.0, 0.0)
    position = jnp.sum(same, axis=0, keepdims=True)
    return row[0:1, :] * float(SLOT) + position


def pack_kernel(group_ref, q_ref, k_ref, v_ref, out_ref, pick_ref):
    slots = GROUPS * SLOT
    rows = q_ref.shape[0]

    @pl.when(pl.program_id(0) == 0)
    def _():
        target = slot_targets(group_ref[...])
        slot = lax.broadcasted_iota(jnp.int32, (slots, rows), 0).astype(jnp.float32)
        pick_ref[...] = jnp.where(slot == target, 1.0, 0.0).astype(jnp.bfloat16)

    pick = pick_ref[...]

    def moved(x):
        return jnp.dot(pick, x, preferred_element_type=jnp.float32)

    def laid(x):
        return x.reshape(GROUPS, SLOT, x.shape[1]).astype(jnp.bfloat16)

    empty = (1.0 - jnp.sum(pick.astype(jnp.float32), axis=1, keepdims=True)) * EMPTY
    for j in range(STEP):
        head = slice(j * HEAD, (j + 1) * HEAD)
        out_ref[j, :, :, 0:QW] = laid(moved(q_ref[:, j * QW : (j + 1) * QW]))
        out_ref[j, :, :, QW : QW + HEAD] = laid(moved(k_ref[:, head]))
        out_ref[j, :, :, QW + HEAD :] = laid(moved(v_ref[:, head]) + empty)


def pack(group, q, k, v):
    rows = q.shape[0]
    return pl.pallas_call(
        pack_kernel,
        grid=(KV_HEADS // STEP,),
        in_specs=[
            pl.BlockSpec((1, rows), lambda j: (0, 0)),
            pl.BlockSpec((rows, STEP * QW), lambda j: (0, j)),
            pl.BlockSpec((rows, STEP * HEAD), lambda j: (0, j)),
            pl.BlockSpec((rows, STEP * HEAD), lambda j: (0, j)),
        ],
        out_specs=pl.BlockSpec((STEP, GROUPS, SLOT, ROW_W), lambda j: (j, 0, 0, 0)),
        out_shape=jax.ShapeDtypeStruct((KV_HEADS, GROUPS, SLOT, ROW_W), jnp.bfloat16),
        scratch_shapes=[pltpu.VMEM((GROUPS * SLOT, rows), jnp.bfloat16)],
        compiler_params=pltpu.CompilerParams(vmem_limit_bytes=GRANT),
        name="pack",
    )(*(pltpu.with_memory_space_constraint(x, pltpu.HBM) for x in (group, q, k, v)))


def unpack_kernel(group_ref, o_ref, out_ref, pick_ref):
    slots = GROUPS * SLOT
    rows = out_ref.shape[0]

    @pl.when(pl.program_id(0) == 0)
    def _():
        target = slot_targets(group_ref[...])
        slot = lax.broadcasted_iota(jnp.int32, (slots, rows), 0).astype(jnp.float32)
        pick_ref[...] = jnp.transpose(jnp.where(slot == target, 1.0, 0.0)).astype(jnp.bfloat16)

    for j in range(STEP):
        x = o_ref[j].reshape(slots, QW)
        out_ref[:, j * QW : (j + 1) * QW] = jnp.dot(
            pick_ref[...], x, preferred_element_type=jnp.float32
        ).astype(jnp.bfloat16)


def unpack(group, o):
    rows = group.shape[1]
    return pl.pallas_call(
        unpack_kernel,
        grid=(KV_HEADS // STEP,),
        in_specs=[
            pl.BlockSpec((1, rows), lambda j: (0, 0)),
            pl.BlockSpec((STEP, GROUPS, SLOT, QW), lambda j: (j, 0, 0, 0)),
        ],
        out_specs=pl.BlockSpec((rows, STEP * QW), lambda j: (0, j)),
        out_shape=jax.ShapeDtypeStruct((rows, KV_HEADS * QW), jnp.bfloat16),
        scratch_shapes=[pltpu.VMEM((rows, GROUPS * SLOT), jnp.bfloat16)],
        compiler_params=pltpu.CompilerParams(vmem_limit_bytes=GRANT),
        name="unpack",
    )(group, o)


def attend_kernel(len_ref, q_ref, k_ref, v_ref, o_ref, feat_ref, mask_ref, ahead_ref, vt_ref, s_ref):
    count = k_ref.shape[0]
    step = pl.program_id(0)

    def joined(ref, b):
        lows = [
            c * PART + b * ROWS + half * NEAR for half in range(2) for c in range(CTX)
        ]
        return jnp.concatenate([ref[low : low + NEAR, :] for low in lows], axis=0)

    @pl.when(step == 0)
    def _():
        first_len = len_ref[0, 0].astype(jnp.float32)
        shape = (GROUPS, SLOT, HEAD)
        lane = lax.broadcasted_iota(jnp.int32, shape, 2).astype(jnp.float32)
        slot = lax.broadcasted_iota(jnp.int32, shape, 1).astype(jnp.float32)
        value = v_ref[...].astype(jnp.float32)
        used = [
            jnp.broadcast_to(
                jnp.where(part.reshape(shape)[:, :, 0:1] < 0.5 * EMPTY, 1.0, 0.0), shape
            )
            for part in (value[c * PART : (c + 1) * PART] for c in range(CTX))
        ]
        slots_of = jnp.where(
            lax.broadcasted_iota(jnp.int32, (GROUPS, PART), 0)
            == lax.broadcasted_iota(jnp.int32, (GROUPS, PART), 1) // SLOT,
            1.0,
            0.0,
        ).astype(jnp.bfloat16)
        number = [
            jnp.dot(
                slots_of,
                u.reshape(PART, HEAD).astype(jnp.bfloat16),
                preferred_element_type=jnp.float32,
            )
            for u in used
        ]
        before = jnp.where(
            lax.broadcasted_iota(jnp.int32, (GROUPS, GROUPS), 0)
            > lax.broadcasted_iota(jnp.int32, (GROUPS, GROUPS), 1),
            1.0,
            0.0,
        )
        base = jnp.dot(
            before.astype(jnp.bfloat16),
            sum(number).astype(jnp.bfloat16),
            preferred_element_type=jnp.float32,
        )
        for c in range(CTX):
            rank = base[:, None, :] + slot
            base = base + number[c]
            code = jnp.where(used[c] > 0.5, jnp.where(rank < first_len, 0.0, 1.0), 2.0)
            hit = lane == code
            at = slice(c * PART, (c + 1) * PART)
            feat_ref[at, :] = jnp.where(hit, 1.0, 0.0).reshape(PART, HEAD).astype(jnp.bfloat16)
            mask_ref[at, :] = jnp.where(hit, 0.0, -FAR).reshape(PART, HEAD).astype(jnp.bfloat16)
        u = lax.broadcasted_iota(jnp.int32, (HALF, SIDE), 0)
        u_order = u % NEAR // SLOT * (CTX * SLOT) + u // NEAR * SLOT + u % SLOT
        t = lax.broadcasted_iota(jnp.int32, (1, LANES), 1)
        t_order = t // SIDE * (HALF) + t % NEAR // SLOT * (CTX * SLOT) + t % SLOT
        ahead_ref[...] = (jnp.concatenate([u_order, u_order], axis=1) - t_order).astype(
            jnp.float32
        )
        for b in range(BLOCKS):
            vt_ref[0:HEAD, b * KEYS : (b + 1) * KEYS] = jnp.transpose(joined(value, b)).astype(
                jnp.bfloat16
            )
        vt_ref[HEAD:, :] = jnp.where(
            lax.broadcasted_iota(jnp.int32, (VALUE_ROWS - HEAD, count), 0) == 0, 1.0, 0.0
        ).astype(jnp.bfloat16)

    scale = math.log2(math.e) / math.sqrt(HEAD)
    bias = jnp.where(ahead_ref[...] <= (step * SLOT).astype(jnp.float32), 0.0, -2.0 * FAR)

    queries = []
    for i in range(BLOCKS):
        pieces = []
        for half in range(2):
            at = slice(half * NEAR, (half + 1) * NEAR)
            mask = mask_ref[
                pl.ds(pl.multiple_of(step * PART + i * ROWS + half * NEAR, NEAR), NEAR), :
            ]
            pieces += [
                jnp.concatenate([q_ref[0, i, at, h * HEAD : (h + 1) * HEAD], mask], axis=1)
                for h in range(PER_KV)
            ]
        queries.append(jnp.concatenate(pieces, axis=0))

    def place(i, b):
        return i * (i + 1) // 2 + b

    def product(key, query):
        return lax.dot_general(
            key, query, (((1,), (1,)), ((), ())), preferred_element_type=jnp.float32
        )

    for b in range(BLOCKS):
        key = jnp.concatenate([joined(k_ref, b), joined(feat_ref, b)], axis=1)
        s_ref[place(b, b), 0:HALF, :] = product(key[0:HALF], queries[b]) + bias
        s_ref[place(b, b), HALF:, SIDE:] = product(key[HALF:], queries[b][SIDE:]) + bias[:, 0:SIDE]
        for i in range(b + 1, BLOCKS):
            s_ref[place(i, b)] = product(key, queries[i])
    for i in range(BLOCKS):
        top = jnp.max(s_ref[place(i, i), 0:HALF, :], axis=0, keepdims=True)
        for b in range(i):
            top = jnp.maximum(top, jnp.max(s_ref[place(i, b)], axis=0, keepdims=True))
        late = jnp.max(s_ref[place(i, i), HALF:, SIDE:], axis=0, keepdims=True)
        late = jnp.maximum(top[:, SIDE:], late)
        top = jnp.concatenate([top[:, 0:SIDE], late], axis=1)

        def part(s, top, low):
            w = jnp.exp2((s - top) * scale).astype(jnp.bfloat16)
            return jnp.dot(
                vt_ref[:, low : low + s.shape[0]], w, preferred_element_type=jnp.float32
            )

        acc = part(s_ref[place(i, i), 0:HALF, :], top, i * KEYS)
        for b in range(i):
            acc = acc + part(s_ref[place(i, b)], top, b * KEYS)
        more = part(s_ref[place(i, i), HALF:, SIDE:], late, i * KEYS + HALF)
        acc = jnp.concatenate([acc[:, 0:SIDE], acc[:, SIDE:] + more], axis=1)
        out = jnp.transpose(acc[0:HEAD] * (1.0 / acc[HEAD : HEAD + 1])).astype(jnp.bfloat16)
        for half in range(2):
            for h in range(PER_KV):
                low = half * SIDE + h * NEAR
                o_ref[0, i, half * NEAR : (half + 1) * NEAR, h * HEAD : (h + 1) * HEAD] = out[
                    low : low + NEAR
                ]


def attend(lengths, rows):
    count = rows.shape[0]
    tile = pl.BlockSpec((1, BLOCKS, ROWS, QW), lambda c: (c, 0, 0, 0))
    out = pl.pallas_call(
        attend_kernel,
        grid=(CTX,),
        in_specs=[
            pl.BlockSpec(memory_space=pltpu.SMEM),
            tile,
            pl.BlockSpec((count, HEAD), lambda i: (0, PER_KV)),
            pl.BlockSpec((count, HEAD), lambda i: (0, PER_KV + 1)),
        ],
        out_specs=tile,
        out_shape=jax.ShapeDtypeStruct((CTX, BLOCKS, ROWS, QW), jnp.bfloat16),
        scratch_shapes=[
            pltpu.VMEM((count, HEAD), jnp.bfloat16),
            pltpu.VMEM((count, HEAD), jnp.bfloat16),
            pltpu.VMEM((HALF, LANES), jnp.float32),
            pltpu.VMEM((VALUE_ROWS, count), jnp.bfloat16),
            pltpu.VMEM((BLOCKS * (BLOCKS + 1) // 2, KEYS, LANES), jnp.float32),
        ],
        compiler_params=pltpu.CompilerParams(vmem_limit_bytes=GRANT),
        name="attend",
    )(lengths, rows.reshape(CTX, BLOCKS, ROWS, ROW_W), rows, rows)
    return out.reshape(count, QW)


def body(query_rows, key_rows, token_values, group_of_row, doc_lengths):
    devices = lax.axis_size("dp") * lax.axis_size("ctx")
    group = group_of_row.reshape(1, group_of_row.shape[0])
    packed = pack(group, query_rows, key_rows, token_values)
    arrived = lax.all_to_all(
        packed.reshape(devices, SLOT, ROW_W), ("ctx", "dp"), split_axis=0, concat_axis=0, tiled=True
    )
    result = attend(doc_lengths, arrived.reshape(devices * SLOT, ROW_W))
    returned = lax.all_to_all(
        result.reshape(devices, SLOT, QW), ("ctx", "dp"), split_axis=0, concat_axis=0, tiled=True
    )
    return unpack(group, returned.reshape(KV_HEADS, GROUPS, SLOT, QW))


def solution(mesh):
    rows = P(("dp", "ctx"), None)
    return jax.shard_map(
        body,
        mesh=mesh,
        in_specs=(rows, rows, rows, rows, P("dp", None)),
        out_specs=rows,
        check_vma=False,
    )
```

```python
import math

import jax
import jax.numpy as jnp
from jax import lax
from jax.experimental import pallas as pl
from jax.experimental.pallas import tpu as pltpu
from jax.sharding import PartitionSpec as P

KV_HEADS = 8
HEAD = 128
PER_KV = 4
GROUPS = 32
SLOT = 8
QW = PER_KV * HEAD
ROW_W = QW + 2 * HEAD
EMPTY = 64.0
FAR = 16384.0
BLOCKS = 4
KEYS = 512
ROWS = 64
LANES = PER_KV * ROWS
CTX = 8
PART = BLOCKS * ROWS
NEAR = ROWS // 2
HALF = KEYS // 2
SIDE = LANES // 2
GRANT = 24 << 20
VALUE_ROWS = HEAD + 16
STEP = 4


def slot_targets(group_row):
    rows = group_row.shape[1]
    row = jnp.broadcast_to(group_row.astype(jnp.float32), (rows, rows))
    col = jnp.transpose(row)
    earlier = lax.broadcasted_iota(jnp.int32, (rows, rows), 0) < lax.broadcasted_iota(
        jnp.int32, (rows, rows), 1
    )
    same = jnp.where((col == row) & earlier, 1.0, 0.0)
    position = jnp.sum(same, axis=0, keepdims=True)
    return row[0:1, :] * float(SLOT) + position


def pack_kernel(group_ref, q_ref, k_ref, v_ref, out_ref, pick_ref):
    slots = GROUPS * SLOT
    rows = q_ref.shape[0]

    @pl.when(pl.program_id(0) == 0)
    def _():
        target = slot_targets(group_ref[...])
        slot = lax.broadcasted_iota(jnp.int32, (slots, rows), 0).astype(jnp.float32)
        pick_ref[...] = jnp.where(slot == target, 1.0, 0.0).astype(jnp.bfloat16)

    pick = pick_ref[...]

    def moved(x):
        return jnp.dot(pick, x, preferred_element_type=jnp.float32)

    def laid(x):
        return x.reshape(GROUPS, SLOT, x.shape[1]).astype(jnp.bfloat16)

    empty = (1.0 - jnp.sum(pick.astype(jnp.float32), axis=1, keepdims=True)) * EMPTY
    for j in range(STEP):
        head = slice(j * HEAD, (j + 1) * HEAD)
        out_ref[j, :, :, 0:QW] = laid(moved(q_ref[:, j * QW : (j + 1) * QW]))
        out_ref[j, :, :, QW : QW + HEAD] = laid(moved(k_ref[:, head]))
        out_ref[j, :, :, QW + HEAD :] = laid(moved(v_ref[:, head]) + empty)


def pack(group, q, k, v):
    rows = q.shape[0]
    return pl.pallas_call(
        pack_kernel,
        grid=(KV_HEADS // STEP,),
        in_specs=[
            pl.BlockSpec((1, rows), lambda j: (0, 0)),
            pl.BlockSpec((rows, STEP * QW), lambda j: (0, j)),
            pl.BlockSpec((rows, STEP * HEAD), lambda j: (0, j)),
            pl.BlockSpec((rows, STEP * HEAD), lambda j: (0, j)),
        ],
        out_specs=pl.BlockSpec((STEP, GROUPS, SLOT, ROW_W), lambda j: (j, 0, 0, 0)),
        out_shape=jax.ShapeDtypeStruct((KV_HEADS, GROUPS, SLOT, ROW_W), jnp.bfloat16),
        scratch_shapes=[pltpu.VMEM((GROUPS * SLOT, rows), jnp.bfloat16)],
        compiler_params=pltpu.CompilerParams(vmem_limit_bytes=GRANT),
        name="pack",
    )(*(pltpu.with_memory_space_constraint(x, pltpu.HBM) for x in (group, q, k, v)))


def unpack_kernel(group_ref, o_ref, out_ref, pick_ref):
    slots = GROUPS * SLOT
    rows = out_ref.shape[0]

    @pl.when(pl.program_id(0) == 0)
    def _():
        target = slot_targets(group_ref[...])
        slot = lax.broadcasted_iota(jnp.int32, (slots, rows), 0).astype(jnp.float32)
        pick_ref[...] = jnp.transpose(jnp.where(slot == target, 1.0, 0.0)).astype(jnp.bfloat16)

    for j in range(STEP):
        x = o_ref[j].reshape(slots, QW)
        out_ref[:, j * QW : (j + 1) * QW] = jnp.dot(
            pick_ref[...], x, preferred_element_type=jnp.float32
        ).astype(jnp.bfloat16)


def unpack(group, o):
    rows = group.shape[1]
    return pl.pallas_call(
        unpack_kernel,
        grid=(KV_HEADS // STEP,),
        in_specs=[
            pl.BlockSpec((1, rows), lambda j: (0, 0)),
            pl.BlockSpec((STEP, GROUPS, SLOT, QW), lambda j: (j, 0, 0, 0)),
        ],
        out_specs=pl.BlockSpec((rows, STEP * QW), lambda j: (0, j)),
        out_shape=jax.ShapeDtypeStruct((rows, KV_HEADS * QW), jnp.bfloat16),
        scratch_shapes=[pltpu.VMEM((rows, GROUPS * SLOT), jnp.bfloat16)],
        compiler_params=pltpu.CompilerParams(vmem_limit_bytes=GRANT),
        name="unpack",
    )(group, o)


def attend_kernel(len_ref, q_ref, k_ref, v_ref, o_ref, feat_ref, mask_ref, ahead_ref, vt_ref, s_ref):
    count = k_ref.shape[0]
    step = pl.program_id(0)

    def joined(ref, b):
        lows = [
            c * PART + b * ROWS + half * NEAR for half in range(2) for c in range(CTX)
        ]
        return jnp.concatenate([ref[low : low + NEAR, :] for low in lows], axis=0)

    @pl.when(step == 0)
    def _():
        first_len = len_ref[0, 0].astype(jnp.float32)
        shape = (GROUPS, SLOT, HEAD)
        lane = lax.broadcasted_iota(jnp.int32, shape, 2).astype(jnp.float32)
        slot = lax.broadcasted_iota(jnp.int32, shape, 1).astype(jnp.float32)
        value = v_ref[...].astype(jnp.float32)
        used = [
            jnp.broadcast_to(
                jnp.where(part.reshape(shape)[:, :, 0:1] < 0.5 * EMPTY, 1.0, 0.0), shape
            )
            for part in (value[c * PART : (c + 1) * PART] for c in range(CTX))
        ]
        slots_of = jnp.where(
            lax.broadcasted_iota(jnp.int32, (GROUPS, PART), 0)
            == lax.broadcasted_iota(jnp.int32, (GROUPS, PART), 1) // SLOT,
            1.0,
            0.0,
        ).astype(jnp.bfloat16)
        number = [
            jnp.dot(
                slots_of,
                u.reshape(PART, HEAD).astype(jnp.bfloat16),
                preferred_element_type=jnp.float32,
            )
            for u in used
        ]
        before = jnp.where(
            lax.broadcasted_iota(jnp.int32, (GROUPS, GROUPS), 0)
            > lax.broadcasted_iota(jnp.int32, (GROUPS, GROUPS), 1),
            1.0,
            0.0,
        )
        base = jnp.dot(
            before.astype(jnp.bfloat16),
            sum(number).astype(jnp.bfloat16),
            preferred_element_type=jnp.float32,
        )
        for c in range(CTX):
            rank = base[:, None, :] + slot
            base = base + number[c]
            code = jnp.where(used[c] > 0.5, jnp.where(rank < first_len, 0.0, 1.0), 2.0)
            hit = lane == code
            at = slice(c * PART, (c + 1) * PART)
            feat_ref[at, :] = jnp.where(hit, 1.0, 0.0).reshape(PART, HEAD).astype(jnp.bfloat16)
            mask_ref[at, :] = jnp.where(hit, 0.0, -FAR).reshape(PART, HEAD).astype(jnp.bfloat16)
        u = lax.broadcasted_iota(jnp.int32, (HALF, SIDE), 0)
        u_order = u % NEAR // SLOT * (CTX * SLOT) + u // NEAR * SLOT + u % SLOT
        t = lax.broadcasted_iota(jnp.int32, (1, LANES), 1)
        t_order = t // SIDE * (HALF) + t % NEAR // SLOT * (CTX * SLOT) + t % SLOT
        ahead_ref[...] = (jnp.concatenate([u_order, u_order], axis=1) - t_order).astype(
            jnp.float32
        )
        for b in range(BLOCKS):
            vt_ref[0:HEAD, b * KEYS : (b + 1) * KEYS] = jnp.transpose(joined(value, b)).astype(
                jnp.bfloat16
            )
        vt_ref[HEAD:, :] = jnp.where(
            lax.broadcasted_iota(jnp.int32, (VALUE_ROWS - HEAD, count), 0) == 0, 1.0, 0.0
        ).astype(jnp.bfloat16)

    scale = math.log2(math.e) / math.sqrt(HEAD)
    bias = jnp.where(ahead_ref[...] <= (step * SLOT).astype(jnp.float32), 0.0, -2.0 * FAR)

    queries = []
    for i in range(BLOCKS):
        pieces = []
        for half in range(2):
            at = slice(half * NEAR, (half + 1) * NEAR)
            mask = mask_ref[
                pl.ds(pl.multiple_of(step * PART + i * ROWS + half * NEAR, NEAR), NEAR), :
            ]
            pieces += [
                jnp.concatenate([q_ref[0, i, at, h * HEAD : (h + 1) * HEAD], mask], axis=1)
                for h in range(PER_KV)
            ]
        queries.append(jnp.concatenate(pieces, axis=0))

    def place(i, b):
        return i * (i + 1) // 2 + b

    def product(key, query):
        return lax.dot_general(
            key, query, (((1,), (1,)), ((), ())), preferred_element_type=jnp.float32
        )

    for b in range(BLOCKS):
        key = jnp.concatenate([joined(k_ref, b), joined(feat_ref, b)], axis=1)
        s_ref[place(b, b), 0:HALF, :] = product(key[0:HALF], queries[b]) + bias
        s_ref[place(b, b), HALF:, SIDE:] = product(key[HALF:], queries[b][SIDE:]) + bias[:, 0:SIDE]
        for i in range(b + 1, BLOCKS):
            s_ref[place(i, b)] = product(key, queries[i])
    for i in range(BLOCKS):
        top = jnp.max(s_ref[place(i, i), 0:HALF, :], axis=0, keepdims=True)
        for b in range(i):
            top = jnp.maximum(top, jnp.max(s_ref[place(i, b)], axis=0, keepdims=True))
        late = jnp.max(s_ref[place(i, i), HALF:, SIDE:], axis=0, keepdims=True)
        late = jnp.maximum(top[:, SIDE:], late)
        top = jnp.concatenate([top[:, 0:SIDE], late], axis=1)

        def part(s, top, low):
            w = jnp.exp2((s - top) * scale).astype(jnp.bfloat16)
            return jnp.dot(
                vt_ref[:, low : low + s.shape[0]], w, preferred_element_type=jnp.float32
            )

        acc = part(s_ref[place(i, i), 0:HALF, :], top, i * KEYS)
        for b in range(i):
            acc = acc + part(s_ref[place(i, b)], top, b * KEYS)
        more = part(s_ref[place(i, i), HALF:, SIDE:], late, i * KEYS + HALF)
        acc = jnp.concatenate([acc[:, 0:SIDE], acc[:, SIDE:] + more], axis=1)
        out = jnp.transpose(acc[0:HEAD] * (1.0 / acc[HEAD : HEAD + 1])).astype(jnp.bfloat16)
        for half in range(2):
            for h in range(PER_KV):
                low = half * SIDE + h * NEAR
                o_ref[0, i, half * NEAR : (half + 1) * NEAR, h * HEAD : (h + 1) * HEAD] = out[
                    low : low + NEAR
                ]


def attend(lengths, rows):
    count = rows.shape[0]
    tile = pl.BlockSpec((1, BLOCKS, ROWS, QW), lambda c: (c, 0, 0, 0))
    out = pl.pallas_call(
        attend_kernel,
        grid=(CTX,),
        in_specs=[
            pl.BlockSpec(memory_space=pltpu.SMEM),
            tile,
            pl.BlockSpec((count, HEAD), lambda i: (0, PER_KV)),
            pl.BlockSpec((count, HEAD), lambda i: (0, PER_KV + 1)),
        ],
        out_specs=tile,
        out_shape=jax.ShapeDtypeStruct((CTX, BLOCKS, ROWS, QW), jnp.bfloat16),
        scratch_shapes=[
            pltpu.VMEM((count, HEAD), jnp.bfloat16),
            pltpu.VMEM((count, HEAD), jnp.bfloat16),
            pltpu.VMEM((HALF, LANES), jnp.float32),
            pltpu.VMEM((VALUE_ROWS, count), jnp.bfloat16),
            pltpu.VMEM((BLOCKS * (BLOCKS + 1) // 2, KEYS, LANES), jnp.float32),
        ],
        compiler_params=pltpu.CompilerParams(vmem_limit_bytes=GRANT),
        name="attend",
    )(lengths, rows.reshape(CTX, BLOCKS, ROWS, ROW_W), rows, rows)
    return out.reshape(count, QW)


def body(query_rows, key_rows, token_values, group_of_row, doc_lengths):
    devices = lax.axis_size("dp") * lax.axis_size("ctx")
    group = group_of_row.reshape(1, group_of_row.shape[0])
    packed = pack(group, query_rows, key_rows, token_values)
    arrived = lax.all_to_all(
        packed.reshape(devices, SLOT, ROW_W), ("ctx", "dp"), split_axis=0, concat_axis=0, tiled=True
    )
    result = attend(doc_lengths, arrived.reshape(devices * SLOT, ROW_W))
    returned = lax.all_to_all(
        result.reshape(devices, SLOT, QW), ("ctx", "dp"), split_axis=0, concat_axis=0, tiled=True
    )
    return unpack(group, returned.reshape(KV_HEADS, GROUPS, SLOT, QW))


def solution(mesh):
    rows = P(("dp", "ctx"), None)
    return jax.shard_map(
        body,
        mesh=mesh,
        in_specs=(rows, rows, rows, rows, P("dp", None)),
        out_specs=rows,
        check_vma=False,
    )
```
